32 devices in a mesh: sec: 2 (over core), row: 4 (over y, x), nest: 4 (over z).
Axes of the slice: x: 2, y: 2, z: 4, core: 2. Of those that a mesh axis runs over, the one named last changes fastest.
Arguments:
- ocean_state: float32 [2, 3, 256, 512], P('sec', None, 'row', 'nest'), may hold values from -1.2 to 1.2
- face_depth: float32 [2, 2, 256, 512], P('sec', None, 'row', 'nest'), may hold values from 2 to 4
- face_open: int32 [2, 2, 256, 512], P('sec', None, 'row', 'nest'), may hold values 0 or 1
- nest_place: int32 [16], replicated, may hold values from 0 to 95, as said below
- nest_host: int32 [16], replicated, may hold values from 0 to 31, as said below
Outputs:
- final_state: float32 [2, 3, 256, 512], P('sec', None, 'row', 'nest')
The draws below stay inside these ranges and needn't reach their ends.
Inputs may be any that keep to these rules, and one draw needn't show every extreme that they name: `nest_place`: distinct positions; the first and the last position are always covered. `nest_host`: distinct slots; both slots of some device hold a nest; the nest at the first position lives in the last slot and the nest at the last position in the first slot.
All inputs are finite; a program needn't handle non-finite values. No bound on the sum of `face_open` on one device may be relied on, other than what follows from the above.
Results may differ from the reference program's by a relative error of at most 0.00013.
Values sent between devices are 32-bit elements; how exact they have to be, the bound alone decides.
A program may use at most 64 MiB of HBM per device.

```python
import math
import jax
import jax.numpy as jnp
from jax import lax

PH = 8
PW = 32
RR = 4
K = 2
STEPS = 4
NT = 16
SLOTS = 32
NPOS = 6
NESTS = 16
OH = 256
OW = 512
N_ROW = 4
N_NEST = 4


def draw_nest_place(key, part):
    total = NT * NPOS
    inner = jax.random.permutation(jax.random.fold_in(key, 11), total - 2).astype(jnp.int32) + 1
    chosen = jnp.concatenate([jnp.array([0, total - 1], jnp.int32), inner[:NESTS - 2]])
    shuffle = jax.random.permutation(jax.random.fold_in(key, 12), NESTS)
    return chosen[shuffle].astype(jnp.int32)


def draw_nest_host(key, part):
    base_key = jax.random.fold_in(key, 23)
    chosen = jax.random.randint(jax.random.fold_in(base_key, 1), (), 0, NT)
    ordering = jax.random.permutation(jax.random.fold_in(base_key, 2), SLOTS).astype(jnp.int32)
    flagged = (ordering // K == chosen).astype(jnp.int32)
    counter = jnp.arange(SLOTS, dtype=jnp.int32)
    scores = jnp.where(ordering == SLOTS - 1, 0, jnp.where(ordering == 0, 1, (3 - flagged) * SLOTS + counter)).astype(jnp.int32)
    assigned = ordering[jnp.argsort(scores)][:NESTS]
    shuffle = jax.random.permutation(jax.random.fold_in(key, 12), NESTS)
    return assigned[shuffle].astype(jnp.int32)


def plant(values, own_key, least, largest):
    dims = values.shape
    spot = [jax.random.randint(jax.random.fold_in(own_key, axis), (), 0, dims[axis]) for axis in range(len(dims))]
    values = values.at[tuple(spot)].set(least)
    longest = dims.index(max(dims))
    spot[longest] = (spot[longest] + 1) % dims[longest]
    return values.at[tuple(spot)].set(largest)


def block_levels(stream_key, dims, pieces, least, largest):
    gain, own = 1.0, jax.random.fold_in(stream_key, 6)
    for dim, blocks in pieces:
        draws = jnp.exp(jax.random.uniform(jax.random.fold_in(own, dim), (blocks,), jnp.float32, least / len(pieces), largest / len(pieces)))
        gain = gain * jnp.repeat(draws, dims[dim] // blocks).reshape([-1 if axis == dim else 1 for axis in range(len(dims))])
    return gain


def normal_values(stream_key, dims, spread, reach, shards=(), kind=jnp.bfloat16):
    gain = block_levels(stream_key, dims, shards, -0.22, 0.18) if shards else 1.0
    values = jax.random.normal(stream_key, dims, jnp.float32) * spread * gain
    return jnp.minimum(jnp.maximum(values, -reach), reach).astype(kind)


def setup_inputs(seed: int = 0) -> dict:
    keys = jax.random.split(jax.random.key(seed), 6)
    return {
        "ocean_state": normal_values(keys[0], (2, 3, OH, OW), 0.3, 1.2, ((0, 2), (2, 4), (3, 4)), jnp.float32),
        "face_depth": jnp.clip(jnp.exp(math.log(4.0) - 0.6931472 * jax.random.uniform(keys[1], (2, 2, OH, OW), jnp.float32) ** block_levels(keys[1], (2, 2, OH, OW), ((0, 2), (2, 4), (3, 4)), -0.2, 0.2)), 2.0, 4.0),
        "face_open": plant((jax.random.randint(keys[2], (2, 2, OH, OW), 0, 8) < 7).astype(jnp.int32), jax.random.fold_in(keys[2], 1), 0, 1),
        "nest_place": draw_nest_place(jax.random.fold_in(keys[5], 71), 0),
        "nest_host": draw_nest_host(jax.random.fold_in(keys[5], 71), 0),
    }


COURANT = 0.3


def surface_update(surface, eastward, southward, west_ghost, north_ghost):
    east_behind = jnp.concatenate([west_ghost, eastward[..., :-1]], axis=-1)
    south_behind = jnp.concatenate([north_ghost, southward[..., :-1, :]], axis=-2)
    return surface - COURANT * ((eastward - east_behind) + (southward - south_behind))


def flux_update(eastward, southward, new_surface, surface_east, surface_south, depth_east, depth_south, open_east, open_south):
    new_eastward = open_east * (eastward - COURANT * (depth_east + 0.5 * (new_surface + surface_east)) * (surface_east - new_surface))
    new_southward = open_south * (southward - COURANT * (depth_south + 0.5 * (new_surface + surface_south)) * (surface_south - new_surface))
    return new_eastward, new_southward


def restrict(surface, eastward, southward):
    leading = surface.shape[:-2]
    coarse_surface = surface.reshape(leading + (PH, RR, PW, RR)).mean(axis=(-3, -1))
    coarse_east = eastward[..., RR - 1::RR].reshape(leading + (PH, RR, PW)).mean(axis=-2)
    coarse_south = southward[..., RR - 1::RR, :].reshape(leading + (PH, PW, RR)).mean(axis=-1)
    return jnp.stack([coarse_surface, coarse_east, coarse_south], axis=-3)


def to_slots(grid):
    channels = grid.shape[0]
    reshaped = grid.reshape(channels, N_ROW, K, RR * PH, N_NEST, RR * PW).transpose(1, 4, 2, 0, 3, 5)
    return reshaped.reshape(N_ROW * N_NEST * K, channels, RR * PH, RR * PW)


def from_slots(slot_states):
    channels = slot_states.shape[1]
    reshaped = slot_states.reshape(N_ROW, N_NEST, K, channels, RR * PH, RR * PW).transpose(3, 0, 2, 4, 1, 5)
    return reshaped.reshape(channels, N_ROW * K * RR * PH, N_NEST * RR * PW)


def nest_anchors(nest_place):
    positions = K * (RR - 1)
    tile_number = nest_place // positions
    within = nest_place % positions
    band_number = within // (RR - 1)
    column_number = within % (RR - 1)
    first_rows = (tile_number // N_NEST) * (K * RR * PH) + band_number * (RR * PH) + (RR - 1) * PH // 2
    first_cols = (tile_number % N_NEST) * (RR * PW) + PW // 2 + column_number * PW
    return first_rows.astype(jnp.int32), first_cols.astype(jnp.int32)


def gather_strips(outer_grid, first_rows, first_cols):
    def one_nest(row_start, col_start):
        west_flux = lax.dynamic_slice(outer_grid[1], (row_start, col_start - 1), (PH, 1))[:, 0]
        east_level = lax.dynamic_slice(outer_grid[0], (row_start, col_start + PW), (PH, 1))[:, 0]
        north_flux = lax.dynamic_slice(outer_grid[2], (row_start - 1, col_start), (1, PW))[0]
        south_level = lax.dynamic_slice(outer_grid[0], (row_start + PH, col_start), (1, PW))[0]
        return jnp.stack([jnp.concatenate([west_flux, north_flux]), jnp.concatenate([east_level, south_level])])
    return jax.vmap(one_nest)(first_rows, first_cols)


def outer_advance(outer_grid, depth_outer, open_outer):
    grid_rows = outer_grid.shape[1]
    grid_cols = outer_grid.shape[2]
    zero_column = jnp.zeros((grid_rows, 1), jnp.float32)
    zero_row = jnp.zeros((1, grid_cols), jnp.float32)
    new_surface = surface_update(outer_grid[0], outer_grid[1], outer_grid[2], zero_column, zero_row)
    surface_east = jnp.concatenate([new_surface[:, 1:], zero_column], axis=1)
    surface_south = jnp.concatenate([new_surface[1:, :], zero_row], axis=0)
    new_eastward, new_southward = flux_update(outer_grid[1], outer_grid[2], new_surface, surface_east, surface_south, depth_outer[0], depth_outer[1], open_outer[0], open_outer[1])
    return jnp.stack([new_surface, new_eastward, new_southward])


def nest_advance(nest_states, depth_fine, open_fine, old_strips, new_strips):
    surface, eastward, southward = nest_states[:, 0], nest_states[:, 1], nest_states[:, 2]
    for substep in range(1, RR + 1):
        ghost_vals = old_strips + (substep / RR) * (new_strips - old_strips)
        west_ghost = jnp.repeat(ghost_vals[:, 0, :PH], RR, axis=1)[:, :, None]
        north_ghost = jnp.repeat(ghost_vals[:, 0, PH:], RR, axis=1)[:, None, :]
        east_ghost = jnp.repeat(ghost_vals[:, 1, :PH], RR, axis=1)[:, :, None]
        south_ghost = jnp.repeat(ghost_vals[:, 1, PH:], RR, axis=1)[:, None, :]
        new_surface = surface_update(surface, eastward, southward, west_ghost, north_ghost)
        surface_east = jnp.concatenate([new_surface[..., 1:], east_ghost], axis=-1)
        surface_south = jnp.concatenate([new_surface[..., 1:, :], south_ghost], axis=-2)
        eastward, southward = flux_update(eastward, southward, new_surface, surface_east, surface_south, depth_fine[:, 0], depth_fine[:, 1], open_fine[:, 0], open_fine[:, 1])
        surface = new_surface
    return jnp.stack([surface, eastward, southward], axis=1)


def write_back(outer_grid, coarse, first_rows, first_cols):
    def place_one(index, grid):
        return lax.dynamic_update_slice(grid, coarse[index], (jnp.zeros((), jnp.int32), first_rows[index], first_cols[index]))
    return lax.fori_loop(0, coarse.shape[0], place_one, outer_grid)


def reference(ocean_state, face_depth, face_open, nest_place, nest_host):
    outer_grid = ocean_state[0]
    depth_outer = face_depth[0]
    open_outer = face_open[0].astype(jnp.float32)
    slot_states = to_slots(ocean_state[1])
    slot_depth = to_slots(face_depth[1])
    slot_open = to_slots(face_open[1].astype(jnp.float32))
    nest_states = slot_states[nest_host]
    depth_fine = slot_depth[nest_host]
    open_fine = slot_open[nest_host]
    first_rows, first_cols = nest_anchors(nest_place)
    old_strips = gather_strips(outer_grid, first_rows, first_cols)
    for timestep in range(STEPS):
        outer_grid = outer_advance(outer_grid, depth_outer, open_outer)
        new_strips = gather_strips(outer_grid, first_rows, first_cols)
        nest_states = nest_advance(nest_states, depth_fine, open_fine, old_strips, new_strips)
        coarse = restrict(nest_states[:, 0], nest_states[:, 1], nest_states[:, 2])
        outer_grid = write_back(outer_grid, coarse, first_rows, first_cols)
        old_strips = new_strips
    slot_states = slot_states.at[nest_host].set(nest_states)
    return jnp.stack([outer_grid, from_slots(slot_states)])
```

```python
import functools

import jax
import jax.numpy as jnp
from jax import lax
from jax.experimental import pallas as pl
from jax.experimental.pallas import tpu as pltpu
from jax.sharding import PartitionSpec as P

PH = 8
PW = 32
RR = 4
K = 2
STEPS = 4
NPOS = K * (RR - 1)
COURANT = 0.3
HIGHEST = lax.Precision.HIGHEST
MESH = pl.DeviceIdType.MESH
FINE_ROWS = RR * PH
TOP = (RR - 1) * PH // 2
LEFT = PW // 2


def iota(shape, dim):
    return lax.broadcasted_iota(jnp.int32, shape, dim)


def new_level(surface, eastward, southward, west_ghost, north_ghost):
    rows, cols = iota(surface.shape, 0), iota(surface.shape, 1)
    east_behind = jnp.where(cols == 0, west_ghost, pltpu.roll(eastward, 1, 1))
    south_behind = jnp.where(rows == 0, north_ghost, pltpu.roll(southward, 1, 0))
    return surface - COURANT * ((eastward - east_behind) + (southward - south_behind))


def new_fluxes(eastward, southward, level, east_ghost, south_ghost, depth, opened):
    height, width = level.shape
    rows, cols = iota(level.shape, 0), iota(level.shape, 1)
    level_east = jnp.where(cols == width - 1, east_ghost, pltpu.roll(level, width - 1, 1))
    level_south = jnp.where(rows == height - 1, south_ghost, pltpu.roll(level, height - 1, 0))
    east = opened[0] * (
        eastward - COURANT * (depth[0] + 0.5 * (level + level_east)) * (level_east - level)
    )
    south = opened[1] * (
        southward - COURANT * (depth[1] + 0.5 * (level + level_south)) * (level_south - level)
    )
    return east, south


def dot(a, b):
    return jnp.dot(a, b, precision=HIGHEST, preferred_element_type=jnp.float32)


def pack_strips(tmp):
    width = tmp.shape[2]
    lane, sub = iota((PH, width), 1), iota((PH, width), 0)
    block = jnp.zeros((PH, width), jnp.float32)
    span = (RR - 1) * PW
    inner = (lane >= LEFT) & (lane < LEFT + span)
    for band in range(K):
        first = band * FINE_ROWS + TOP
        east8 = tmp[1, first : first + PH, :]
        level8 = tmp[0, first : first + PH, :]
        for j in range(RR - 1):
            column = LEFT + j * PW
            west_lane = band * 2 * (RR - 1) + j
            east_lane = west_lane + RR - 1
            block = jnp.where(
                lane == west_lane, pltpu.roll(east8, (west_lane - column + 1) % width, 1), block
            )
            block = jnp.where(
                lane == east_lane, pltpu.roll(level8, (east_lane - column - PW) % width, 1), block
            )
        block = jnp.where(inner & (sub == 2 * band), tmp[2, first - 1 : first, :], block)
        block = jnp.where(inner & (sub == 2 * band + 1), tmp[0, first + PH : first + PH + 1, :], block)
    return block


def kernel(
    n_row,
    n_nest,
    place_ref,
    host_ref,
    state_ref,
    depth_ref,
    open_ref,
    out_ref,
    st,
    tmp,
    strips_out,
    strips_in,
    ret_out,
    ret_in,
    east_out,
    south_out,
    level_out,
    west_in,
    north_in,
    east_in,
    south_in,
    spread,
    ghosts,
    strips_now,
    ret_now,
    strip_send,
    strip_recv,
    ret_send,
    ret_recv,
    halo_send,
    halo_recv,
):
    tiles = n_row * n_nest
    nests = place_ref.shape[0]
    sec, row, col = lax.axis_index("sec"), lax.axis_index("row"), lax.axis_index("nest")
    tile = row * n_nest + col
    is_outer = sec == 0
    has_west, has_east = col > 0, col < n_nest - 1
    has_north, has_south = row > 0, row < n_row - 1
    west, east = (sec, row, col - 1), (sec, row, col + 1)
    north, south = (sec, row - 1, col), (sec, row + 1, col)
    links = ((has_west, west), (has_east, east), (has_north, north), (has_south, south))
    height, width = state_ref.shape[2], state_ref.shape[3]

    barrier = pltpu.get_barrier_semaphore()

    @pl.loop(0, tiles)
    def _(i):
        t = lax.rem(tile + i, tiles)
        pl.semaphore_signal(
            barrier, inc=1, device_id=(1 - sec, t // n_nest, lax.rem(t, n_nest)), device_id_type=MESH
        )

    def send_all(src, dst_of, send_sem, recv_sem):
        @pl.loop(0, tiles)
        def _(i):
            t = lax.rem(tile + i + 1, tiles)
            pltpu.make_async_remote_copy(
                src_ref=src,
                dst_ref=dst_of,
                send_sem=send_sem,
                recv_sem=recv_sem,
                device_id=(1 - sec, t // n_nest, lax.rem(t, n_nest)),
                device_id_type=MESH,
            ).start()

    def wait_all(whole, sem):
        pltpu.make_async_copy(whole, whole, sem).wait()

    @pl.when(is_outer)
    def _():
        for present, device in links:

            @pl.when(present)
            def _():
                pl.semaphore_signal(barrier, inc=1, device_id=device, device_id_type=MESH)

        st[...] = state_ref[0]
        depth = [depth_ref[0, i] for i in range(2)]
        opened = [open_ref[0, i].astype(jnp.float32) for i in range(2)]
        slots, covers = [], []
        for p in range(NPOS):
            slot, cover = jnp.int32(0), jnp.int32(0)
            for n in range(nests):
                hit = place_ref[n] == tile * NPOS + p
                slot = jnp.where(hit, host_ref[n], slot)
                cover = jnp.where(hit, 1, cover)
            slots.append(slot)
            covers.append(cover)
        zero_block = jnp.zeros((height, width), jnp.float32)
        for present, buffer in (
            (has_west, west_in),
            (has_east, east_in),
            (has_north, north_in),
            (has_south, south_in),
        ):

            @pl.when(jnp.logical_not(present))
            def _():
                for s in range(STEPS):
                    buffer[s] = jnp.zeros(buffer.shape[1:], jnp.float32)

        peers = jnp.int32(tiles)
        for present, _device in links:
            peers = peers + jnp.where(present, 1, 0)
        pl.semaphore_wait(barrier, peers)

        strips_out[0] = pack_strips(st)
        send_all(strips_out.at[0], strips_in.at[0, tile], strip_send.at[0], strip_recv.at[0])

        def halo(s, kind, src, dst, device):
            return pltpu.make_async_remote_copy(
                src_ref=src,
                dst_ref=dst,
                send_sem=halo_send.at[s, kind],
                recv_sem=halo_recv.at[s, kind],
                device_id=device,
                device_id_type=MESH,
            )

        @pl.loop(0, STEPS)
        def _(s):
            surface, eastward, southward = st[0], st[1], st[2]
            level = new_level(surface, eastward, southward, 0.0, 0.0)
            fluxes = new_fluxes(eastward, southward, level, 0.0, 0.0, depth, opened)
            tmp[0] = level
            tmp[1] = fluxes[0]
            tmp[2] = fluxes[1]
            strips_out[s + 1] = pack_strips(tmp)
            send_all(
                strips_out.at[s + 1],
                strips_in.at[s + 1, tile],
                strip_send.at[s + 1],
                strip_recv.at[s + 1],
            )

            east_out[s] = eastward
            south_out[s] = southward[height - 8 :]
            to_east = halo(s, 0, east_out.at[s], west_in.at[s], east)
            to_south = halo(s, 1, south_out.at[s], north_in.at[s], south)
            to_west = halo(s, 2, level_out.at[s], east_in.at[s], west)
            to_north = halo(s, 3, level_out.at[s, pl.ds(0, 8)], south_in.at[s], north)

            @pl.when(has_east)
            def _():
                to_east.start()

            @pl.when(has_south)
            def _():
                to_south.start()

            @pl.when(has_west)
            def _():
                to_east.wait_recv()

            @pl.when(has_north)
            def _():
                to_south.wait_recv()

            level = new_level(
                surface,
                eastward,
                southward,
                west_in[s][:, width - 1 : width],
                north_in[s][7:8, :],
            )
            level_out[s] = level

            @pl.when(has_west)
            def _():
                to_west.start()

            @pl.when(has_north)
            def _():
                to_north.start()

            @pl.when(has_east)
            def _():
                to_west.wait_recv()

            @pl.when(has_south)
            def _():
                to_north.wait_recv()

            fluxes = new_fluxes(
                eastward, southward, level, east_in[s][:, 0:1], south_in[s][0:1, :], depth, opened
            )
            st[0] = level
            st[1] = fluxes[0]
            st[2] = fluxes[1]

            wait_all(ret_in.at[s], ret_recv.at[s])
            ret_now[...] = ret_in[s]
            lane = iota((PH, width), 1)
            for band in range(K):
                first = band * FINE_ROWS + TOP
                merged = [st[f, first : first + PH, :] for f in range(3)]
                for j in range(RR - 1):
                    p = band * (RR - 1) + j
                    column = LEFT + j * PW
                    block = ret_now[slots[p]]
                    mask = (
                        (lane >= column)
                        & (lane < column + PW)
                        & (jnp.full((PH, width), covers[p], jnp.int32) > 0)
                    )
                    for f in range(3):
                        shifted = pltpu.roll(block, (column - f * PW) % width, 1)
                        merged[f] = jnp.where(mask, shifted, merged[f])
                for f in range(3):
                    st[f, first : first + PH, :] = merged[f]

        out_ref[0] = st[...]

        for s in range(STEPS):

            @pl.when(has_east)
            def _():
                halo(s, 0, east_out.at[s], west_in.at[s], east).wait_send()

            @pl.when(has_south)
            def _():
                halo(s, 1, south_out.at[s], north_in.at[s], south).wait_send()

            @pl.when(has_west)
            def _():
                halo(s, 2, level_out.at[s], east_in.at[s], west).wait_send()

            @pl.when(has_north)
            def _():
                halo(s, 3, level_out.at[s, pl.ds(0, 8)], south_in.at[s], north).wait_send()

        for s in range(STEPS + 1):
            wait_all(strips_in.at[s], strip_send.at[s])

    @pl.when(jnp.logical_not(is_outer))
    def _():
        st[...] = state_ref[0]
        spots, lives = [], []
        for k in range(K):
            spot, live = jnp.int32(0), jnp.int32(0)
            for n in range(nests):
                hit = host_ref[n] == tile * K + k
                spot = jnp.where(hit, place_ref[n], spot)
                live = jnp.where(hit, 1, live)
            spots.append(spot)
            lives.append(live)
        homes = [spot // NPOS for spot in spots]
        bands = [lax.rem(spot, NPOS) // (RR - 1) for spot in spots]
        columns = [lax.rem(spot, RR - 1) for spot in spots]
        for k in range(K):
            source = iota((width, width), 0)
            fine = iota((width, width), 1)
            wanted = LEFT + columns[k] * PW + fine // RR
            spread[k] = (source == wanted).astype(jnp.float32)
        grow = (iota((FINE_ROWS, PH), 0) // RR == iota((FINE_ROWS, PH), 1)).astype(jnp.float32)
        gather_from = iota((3 * width, width), 0)
        gather_to = iota((3 * width, width), 1)
        field, lane_in = gather_from // width, lax.rem(gather_from, width)
        weight = jnp.where(
            field == 1, jnp.where(lax.rem(lane_in, RR) == RR - 1, 1.0, 0.0), 1.0 / RR
        )
        gather = jnp.where(gather_to == field * PW + lane_in // RR, weight, 0.0)
        shrink_row = iota((2 * PH, FINE_ROWS), 0)
        shrink_from = iota((2 * PH, FINE_ROWS), 1)
        shrink = jnp.where(
            shrink_row < PH,
            jnp.where(shrink_from // RR == shrink_row, 1.0 / RR, 0.0),
            jnp.where(shrink_from == (shrink_row - PH) * RR + RR - 1, 1.0, 0.0),
        )

        def side_ghosts(block, k):
            lane, sub = iota((PH, width), 1), iota((PH, width), 0)
            tall_lane = iota((FINE_ROWS, width), 1)
            tall = dot(grow, block)
            wide = dot(block, spread[k])
            west_lane = bands[k] * (2 * (RR - 1)) + columns[k]
            west = jnp.sum(jnp.where(tall_lane == west_lane, tall, 0.0), axis=1, keepdims=True)
            east = jnp.sum(
                jnp.where(tall_lane == west_lane + (RR - 1), tall, 0.0), axis=1, keepdims=True
            )
            north = jnp.sum(jnp.where(sub == 2 * bands[k], wide, 0.0), axis=0, keepdims=True)
            south = jnp.sum(jnp.where(sub == 2 * bands[k] + 1, wide, 0.0), axis=0, keepdims=True)
            return west, north, east, south

        def keep(k, sides):
            west, north, east, south = sides
            lane = iota((FINE_ROWS, width), 1)
            ghosts[k, 0:FINE_ROWS] = jnp.where(lane == 0, west, east)
            ghosts[k, FINE_ROWS : FINE_ROWS + 8] = jnp.where(
                iota((8, width), 0) == 0, north, south
            )

        def kept(k):
            return (
                ghosts[k, 0:FINE_ROWS][:, 0:1],
                ghosts[k, FINE_ROWS : FINE_ROWS + 1],
                ghosts[k, 0:FINE_ROWS][:, 1:2],
                ghosts[k, FINE_ROWS + 1 : FINE_ROWS + 2],
            )

        pl.semaphore_wait(barrier, tiles)
        wait_all(strips_in.at[0], strip_recv.at[0])
        strips_now[...] = strips_in[0]
        for k in range(K):
            keep(k, side_ghosts(strips_now[homes[k]], k))

        @pl.loop(0, STEPS)
        def _(s):
            wait_all(strips_in.at[s + 1], strip_recv.at[s + 1])
            strips_now[...] = strips_in[s + 1]
            for k in range(K):
                slot = pl.ds(k * FINE_ROWS, FINE_ROWS)
                old = kept(k)
                new = side_ghosts(strips_now[homes[k]], k)
                surface, eastward, southward = st[0, slot], st[1, slot], st[2, slot]
                depth = [depth_ref[0, i, slot] for i in range(2)]
                opened = [open_ref[0, i, slot].astype(jnp.float32) for i in range(2)]
                for m in range(1, RR + 1):
                    west_g, north_g, east_g, south_g = [
                        a + (m / RR) * (b - a) for a, b in zip(old, new)
                    ]
                    surface = new_level(surface, eastward, southward, west_g, north_g)
                    eastward, southward = new_fluxes(
                        eastward, southward, surface, east_g, south_g, depth, opened
                    )
                st[0, slot] = surface
                st[1, slot] = eastward
                st[2, slot] = southward
                packed = dot(jnp.concatenate([surface, eastward, southward], axis=1), gather)
                both = dot(shrink, packed)
                ret_out[s, k] = jnp.where(
                    iota((PH, width), 1) < 2 * PW, both[0:PH], both[PH : 2 * PH]
                )
                keep(k, new)
            send_all(ret_out.at[s], ret_in.at[s, pl.ds(tile * K, K)], ret_send.at[s], ret_recv.at[s])

        for k in range(K):
            slot = pl.ds(k * FINE_ROWS, FINE_ROWS)
            live = jnp.full((FINE_ROWS, width), lives[k], jnp.int32) > 0
            for f in range(3):
                out_ref[0, f, slot] = jnp.where(live, st[f, slot], state_ref[0, f, slot])

        for s in range(STEPS):
            wait_all(ret_in.at[s], ret_send.at[s])


def on_device(n_row, n_nest, ocean_state, face_depth, face_open, nest_place, nest_host):
    tiles = n_row * n_nest
    height, width = ocean_state.shape[2:]
    f32 = jnp.float32
    vmem = pl.BlockSpec(memory_space=pltpu.VMEM)
    smem = pl.BlockSpec(memory_space=pltpu.SMEM)
    dma = pltpu.SemaphoreType.DMA
    return pl.pallas_call(
        functools.partial(kernel, n_row, n_nest),
        out_shape=jax.ShapeDtypeStruct(ocean_state.shape, f32),
        in_specs=[smem, smem, vmem, vmem, vmem],
        out_specs=vmem,
        scratch_shapes=[
            pltpu.VMEM((3, height, width), f32),
            pltpu.VMEM((3, height, width), f32),
            pltpu.VMEM((STEPS + 1, PH, width), f32),
            pltpu.VMEM((STEPS + 1, tiles, PH, width), f32),
            pltpu.VMEM((STEPS, K, PH, width), f32),
            pltpu.VMEM((STEPS, tiles * K, PH, width), f32),
            pltpu.VMEM((STEPS, height, width), f32),
            pltpu.VMEM((STEPS, 8, width), f32),
            pltpu.VMEM((STEPS, height, width), f32),
            pltpu.VMEM((STEPS, height, width), f32),
            pltpu.VMEM((STEPS, 8, width), f32),
            pltpu.VMEM((STEPS, height, width), f32),
            pltpu.VMEM((STEPS, 8, width), f32),
            pltpu.VMEM((K, width, width), f32),
            pltpu.VMEM((K, FINE_ROWS + 8, width), f32),
            pltpu.VMEM((tiles, PH, width), f32),
            pltpu.VMEM((tiles * K, PH, width), f32),
            dma((STEPS + 1,)),
            dma((STEPS + 1,)),
            dma((STEPS,)),
            dma((STEPS,)),
            dma((STEPS, 4)),
            dma((STEPS, 4)),
        ],
        compiler_params=pltpu.CompilerParams(collective_id=0, has_side_effects=True),
    )(nest_place, nest_host, ocean_state, face_depth, face_open)


def solution(mesh):
    field = P("sec", None, "row", "nest")
    return jax.shard_map(
        functools.partial(on_device, mesh.shape["row"], mesh.shape["nest"]),
        mesh=mesh,
        in_specs=(field, field, field, P(), P()),
        out_specs=field,
        check_vma=False,
    )
```

```python
import functools

import jax
import jax.numpy as jnp
from jax import lax
from jax.experimental import pallas as pl
from jax.experimental.pallas import tpu as pltpu
from jax.sharding import PartitionSpec as P

PH = 8
PW = 32
RR = 4
K = 2
STEPS = 4
NPOS = K * (RR - 1)
COURANT = 0.3
HIGHEST = lax.Precision.HIGHEST
MESH = pl.DeviceIdType.MESH
FINE_ROWS = RR * PH
TOP = (RR - 1) * PH // 2
LEFT = PW // 2
EDGES = ((0, PW - 1), (1, PW - 1), (1, PW - 2), (2, PW - 1), (0, 0), (1, 0), (2, 0))


def iota(shape, dim):
    return lax.broadcasted_iota(jnp.int32, shape, dim)


def new_level(surface, eastward, southward, west_ghost, north_ghost):
    rows, cols = iota(surface.shape, 0), iota(surface.shape, 1)
    east_behind = jnp.where(cols == 0, west_ghost, pltpu.roll(eastward, 1, 1))
    south_behind = jnp.where(rows == 0, north_ghost, pltpu.roll(southward, 1, 0))
    return surface - COURANT * ((eastward - east_behind) + (southward - south_behind))


def new_fluxes(eastward, southward, level, east_ghost, south_ghost, depth, opened):
    height, width = level.shape
    rows, cols = iota(level.shape, 0), iota(level.shape, 1)
    level_east = jnp.where(cols == width - 1, east_ghost, pltpu.roll(level, width - 1, 1))
    level_south = jnp.where(rows == height - 1, south_ghost, pltpu.roll(level, height - 1, 0))
    east = opened[0] * (
        eastward - COURANT * (depth[0] + 0.5 * (level + level_east)) * (level_east - level)
    )
    south = opened[1] * (
        southward - COURANT * (depth[1] + 0.5 * (level + level_south)) * (level_south - level)
    )
    return east, south


def dot(a, b):
    return jnp.dot(a, b, precision=HIGHEST, preferred_element_type=jnp.float32)


def pack_strips(tmp):
    width = tmp.shape[2]
    lane, sub = iota((PH, width), 1), iota((PH, width), 0)
    block = jnp.zeros((PH, width), jnp.float32)
    span = (RR - 1) * PW
    inner = (lane >= LEFT) & (lane < LEFT + span)
    for band in range(K):
        first = band * FINE_ROWS + TOP
        east8 = tmp[1, first : first + PH, :]
        level8 = tmp[0, first : first + PH, :]
        for j in range(RR - 1):
            column = LEFT + j * PW
            west_lane = band * 2 * (RR - 1) + j
            east_lane = west_lane + RR - 1
            block = jnp.where(
                lane == west_lane, pltpu.roll(east8, (west_lane - column + 1) % width, 1), block
            )
            block = jnp.where(
                lane == east_lane, pltpu.roll(level8, (east_lane - column - PW) % width, 1), block
            )
        block = jnp.where(inner & (sub == 2 * band), tmp[2, first - 1 : first, :], block)
        block = jnp.where(inner & (sub == 2 * band + 1), tmp[0, first + PH : first + PH + 1, :], block)
    return block


def pack_ring(sides, lines):
    ref, width = sides[0][0], sides[0][0].shape[-1]
    lane, sub = iota((PH, width), 1), iota((PH, width), 0)
    span = (RR - 1) * PW
    block = jnp.zeros((PH, width), jnp.float32)
    inner = (lane >= LEFT) & (lane < LEFT + span)
    for band in range(K):
        first = band * FINE_ROWS + TOP
        base = band * (LEFT + span)
        for i, (ref, index, shift) in enumerate(sides):
            values = ref[index + (slice(first, first + PH), slice(None))].astype(jnp.float32)
            for j in range(RR - 1):
                target = base + 3 * j + i
                source = LEFT + j * PW + shift
                block = jnp.where(
                    lane == target, pltpu.roll(values, (target - source) % width, 1), block
                )
        for i, (ref, index, shift) in enumerate(lines):
            at = first + shift
            line = ref[index + (slice(at, at + 1), slice(None))].astype(jnp.float32)
            block = jnp.where(inner & (sub == 3 * band + i), line, block)
    return block


def kernel(
    n_row,
    n_nest,
    place_ref,
    host_ref,
    state_ref,
    depth_ref,
    open_ref,
    out_ref,
    st,
    tmp,
    first_out,
    first_in,
    fixed_out,
    fixed_in,
    ring_out,
    ring_in,
    edge_out,
    edge_in,
    ret_out,
    ret_in,
    east_out,
    south_out,
    level_out,
    west_in,
    north_in,
    east_in,
    south_in,
    spread,
    ghosts,
    ring_now,
    edge_now,
    ret_now,
    fixed_terms,
    first_sems,
    fixed_sems,
    ring_send,
    ring_recv,
    edge_send,
    edge_recv,
    ret_send,
    ret_recv,
    halo_send,
    halo_recv,
):
    tiles = n_row * n_nest
    nests = place_ref.shape[0]
    sec, row, col = lax.axis_index("sec"), lax.axis_index("row"), lax.axis_index("nest")
    tile = row * n_nest + col
    is_outer = sec == 0
    has_west, has_east = col > 0, col < n_nest - 1
    has_north, has_south = row > 0, row < n_row - 1
    west, east = (sec, row, col - 1), (sec, row, col + 1)
    north, south = (sec, row - 1, col), (sec, row + 1, col)
    links = ((has_west, west), (has_east, east), (has_north, north), (has_south, south))
    height, width = state_ref.shape[2], state_ref.shape[3]

    barrier = pltpu.get_barrier_semaphore()

    @pl.loop(0, tiles)
    def _(i):
        t = lax.rem(tile + i, tiles)
        pl.semaphore_signal(
            barrier, inc=1, device_id=(1 - sec, t // n_nest, lax.rem(t, n_nest)), device_id_type=MESH
        )

    def send_to(section, count, src, dst, send_sem, recv_sem):
        @pl.loop(0, count)
        def _(i):
            t = lax.rem(tile + i + 1, tiles)
            pltpu.make_async_remote_copy(
                src_ref=src,
                dst_ref=dst,
                send_sem=send_sem,
                recv_sem=recv_sem,
                device_id=(section, t // n_nest, lax.rem(t, n_nest)),
                device_id_type=MESH,
            ).start()

    def send_all(src, dst, send_sem, recv_sem):
        send_to(1 - sec, tiles, src, dst, send_sem, recv_sem)

    def wait_all(whole, sem):
        pltpu.make_async_copy(whole, whole, sem).wait()

    @pl.when(is_outer)
    def _():
        for present, device in links:

            @pl.when(present)
            def _():
                pl.semaphore_signal(barrier, inc=1, device_id=device, device_id_type=MESH)

        st[...] = state_ref[0]
        depth = [depth_ref[0, i] for i in range(2)]
        opened = [open_ref[0, i].astype(jnp.float32) for i in range(2)]
        slots, covers = [], []
        for p in range(NPOS):
            slot, cover = jnp.int32(0), jnp.int32(0)
            for n in range(nests):
                hit = place_ref[n] == tile * NPOS + p
                slot = jnp.where(hit, host_ref[n], slot)
                cover = jnp.where(hit, 1, cover)
            slots.append(slot)
            covers.append(cover)
        zero_block = jnp.zeros((height, width), jnp.float32)
        for present, buffer in (
            (has_west, west_in),
            (has_east, east_in),
            (has_north, north_in),
            (has_south, south_in),
        ):

            @pl.when(jnp.logical_not(present))
            def _():
                for s in range(STEPS):
                    buffer[s] = jnp.zeros(buffer.shape[1:], jnp.float32)

        peers = jnp.int32(tiles)
        for present, _device in links:
            peers = peers + jnp.where(present, 1, 0)
        pl.semaphore_wait(barrier, peers)

        def halo(s, kind, src, dst, device):
            return pltpu.make_async_remote_copy(
                src_ref=src,
                dst_ref=dst,
                send_sem=halo_send.at[s, kind],
                recv_sem=halo_recv.at[s, kind],
                device_id=device,
                device_id_type=MESH,
            )

        @pl.loop(0, STEPS)
        def _(s):
            surface, eastward, southward = st[0], st[1], st[2]
            level = new_level(surface, eastward, southward, 0.0, 0.0)
            fluxes = new_fluxes(eastward, southward, level, 0.0, 0.0, depth, opened)
            tmp[0] = level
            tmp[1] = fluxes[0]
            tmp[2] = fluxes[1]

            @pl.when(s == 0)
            def _():
                first_out[0] = pack_strips(st)
                first_out[1] = pack_strips(tmp)
                send_all(first_out, first_in.at[tile], first_sems.at[0], first_sems.at[1])

            @pl.when(s < STEPS - 1)
            def _():
                cols = iota((height, width), 1)
                rows = iota((height, width), 0)
                east_gap = fluxes[0] - jnp.where(cols == 0, 0.0, pltpu.roll(fluxes[0], 1, 1))
                south_gap = fluxes[1] - jnp.where(rows == 0, 0.0, pltpu.roll(fluxes[1], 1, 0))
                tmp[3] = level - COURANT * (east_gap + south_gap)
                tmp[4] = level - COURANT * (fluxes[0] + south_gap)
                tmp[5] = level - COURANT * (east_gap + fluxes[1])
                ring_out[s] = pack_ring(
                    [(tmp, (3,), -1), (tmp, (1,), -1), (tmp, (4,), PW)],
                    [(tmp, (3,), -1), (tmp, (2,), -1), (tmp, (5,), PH)],
                )
                send_all(ring_out.at[s], ring_in.at[s, tile], ring_send.at[s], ring_recv.at[s])

            @pl.when(s == 0)
            def _():
                fixed_out[...] = pack_ring(
                    [(depth_ref, (0, 0), -1), (open_ref, (0, 0), -1)],
                    [(depth_ref, (0, 1), -1), (open_ref, (0, 1), -1)],
                )
                send_all(fixed_out, fixed_in.at[tile], fixed_sems.at[0], fixed_sems.at[1])

            east_out[s] = eastward
            south_out[s] = southward[height - 8 :]
            to_east = halo(s, 0, east_out.at[s], west_in.at[s], east)
            to_south = halo(s, 1, south_out.at[s], north_in.at[s], south)
            to_west = halo(s, 2, level_out.at[s], east_in.at[s], west)
            to_north = halo(s, 3, level_out.at[s, pl.ds(0, 8)], south_in.at[s], north)

            @pl.when(has_east)
            def _():
                to_east.start()

            @pl.when(has_south)
            def _():
                to_south.start()

            @pl.when(has_west)
            def _():
                to_east.wait_recv()

            @pl.when(has_north)
            def _():
                to_south.wait_recv()

            level = new_level(
                surface,
                eastward,
                southward,
                west_in[s][:, width - 1 : width],
                north_in[s][7:8, :],
            )
            level_out[s] = level

            @pl.when(has_west)
            def _():
                to_west.start()

            @pl.when(has_north)
            def _():
                to_north.start()

            @pl.when(has_east)
            def _():
                to_west.wait_recv()

            @pl.when(has_south)
            def _():
                to_north.wait_recv()

            fluxes = new_fluxes(
                eastward, southward, level, east_in[s][:, 0:1], south_in[s][0:1, :], depth, opened
            )
            st[0] = level
            st[1] = fluxes[0]
            st[2] = fluxes[1]

            wait_all(ret_in.at[s], ret_recv.at[s])
            ret_now[...] = ret_in[s]
            lane = iota((PH, width), 1)
            for band in range(K):
                first = band * FINE_ROWS + TOP
                merged = [st[f, first : first + PH, :] for f in range(3)]
                for j in range(RR - 1):
                    p = band * (RR - 1) + j
                    column = LEFT + j * PW
                    block = ret_now[slots[p]]
                    mask = (
                        (lane >= column)
                        & (lane < column + PW)
                        & (jnp.full((PH, width), covers[p], jnp.int32) > 0)
                    )
                    for f in range(3):
                        shifted = pltpu.roll(block, (column - f * PW) % width, 1)
                        merged[f] = jnp.where(mask, shifted, merged[f])
                for f in range(3):
                    st[f, first : first + PH, :] = merged[f]

        out_ref[0] = st[...]

        for s in range(STEPS):

            @pl.when(has_east)
            def _():
                halo(s, 0, east_out.at[s], west_in.at[s], east).wait_send()

            @pl.when(has_south)
            def _():
                halo(s, 1, south_out.at[s], north_in.at[s], south).wait_send()

            @pl.when(has_west)
            def _():
                halo(s, 2, level_out.at[s], east_in.at[s], west).wait_send()

            @pl.when(has_north)
            def _():
                halo(s, 3, level_out.at[s, pl.ds(0, 8)], south_in.at[s], north).wait_send()

        wait_all(first_in, first_sems.at[0])
        wait_all(fixed_in, fixed_sems.at[0])
        for s in range(STEPS - 1):
            wait_all(ring_in.at[s], ring_send.at[s])

    @pl.when(jnp.logical_not(is_outer))
    def _():
        @pl.loop(0, tiles - 1)
        def _(i):
            t = lax.rem(tile + i + 1, tiles)
            pl.semaphore_signal(
                barrier, inc=1, device_id=(sec, t // n_nest, lax.rem(t, n_nest)), device_id_type=MESH
            )

        st[...] = state_ref[0]
        spots, lives = [], []
        for k in range(K):
            spot, live = jnp.int32(0), jnp.int32(0)
            for n in range(nests):
                hit = host_ref[n] == tile * K + k
                spot = jnp.where(hit, place_ref[n], spot)
                live = jnp.where(hit, 1, live)
            spots.append(spot)
            lives.append(live)
        homes = [spot // NPOS for spot in spots]
        bands = [lax.rem(spot, NPOS) // (RR - 1) for spot in spots]
        columns = [lax.rem(spot, RR - 1) for spot in spots]
        near = []
        for k in range(K):
            pair = []
            for side in (-1, 1):
                inside = (columns[k] + side >= 0) & (columns[k] + side < RR - 1)
                slot, cover = jnp.int32(0), jnp.int32(0)
                for n in range(nests):
                    hit = inside & (place_ref[n] == spots[k] + side)
                    slot = jnp.where(hit, host_ref[n], slot)
                    cover = jnp.where(hit, 1, cover)
                pair.append((slot // K, lax.rem(slot, K), cover))
            near.append(pair)
        for k in range(K):
            source = iota((width, width), 0)
            fine = iota((width, width), 1)
            wanted = LEFT + columns[k] * PW + fine // RR
            spread[k] = (source == wanted).astype(jnp.float32)
        grow = (iota((FINE_ROWS, PH), 0) // RR == iota((FINE_ROWS, PH), 1)).astype(jnp.float32)
        gather_from = iota((3 * width, width), 0)
        gather_to = iota((3 * width, width), 1)
        field, lane_in = gather_from // width, lax.rem(gather_from, width)
        weight = jnp.where(
            field == 1, jnp.where(lax.rem(lane_in, RR) == RR - 1, 1.0, 0.0), 1.0 / RR
        )
        gather = jnp.where(gather_to == field * PW + lane_in // RR, weight, 0.0)
        for i, (f, c) in enumerate(EDGES):
            gather = gather + jnp.where(
                (gather_to == 3 * PW + i) & (field == f) & (lane_in // RR == c), weight, 0.0
            )
        widen_to = iota((width, 3 * width), 1)
        widen = (
            iota((width, 3 * width), 0)
            == (widen_to // width) * PW + lax.rem(widen_to, width) // RR
        ).astype(jnp.float32)
        shrink_row = iota((2 * PH, FINE_ROWS), 0)
        shrink_from = iota((2 * PH, FINE_ROWS), 1)
        shrink = jnp.where(
            shrink_row < PH,
            jnp.where(shrink_from // RR == shrink_row, 1.0 / RR, 0.0),
            jnp.where(shrink_from == (shrink_row - PH) * RR + RR - 1, 1.0, 0.0),
        )

        def side_ghosts(block, k):
            lane, sub = iota((PH, width), 1), iota((PH, width), 0)
            tall_lane = iota((FINE_ROWS, width), 1)
            tall = dot(grow, block)
            wide = dot(block, spread[k])
            west_lane = bands[k] * (2 * (RR - 1)) + columns[k]
            west = jnp.sum(jnp.where(tall_lane == west_lane, tall, 0.0), axis=1, keepdims=True)
            east = jnp.sum(
                jnp.where(tall_lane == west_lane + (RR - 1), tall, 0.0), axis=1, keepdims=True
            )
            north = jnp.sum(jnp.where(sub == 2 * bands[k], wide, 0.0), axis=0, keepdims=True)
            south = jnp.sum(jnp.where(sub == 2 * bands[k] + 1, wide, 0.0), axis=0, keepdims=True)
            return west, north, east, south

        def keep(buffer, k, sides):
            west, north, east, south = sides
            lane = iota((FINE_ROWS, width), 1)
            buffer[k, 0:FINE_ROWS] = jnp.where(lane == 0, west, east)
            buffer[k, FINE_ROWS : FINE_ROWS + 8] = jnp.where(
                iota((8, width), 0) == 0, north, south
            )

        def kept(buffer, k):
            return (
                buffer[k, 0:FINE_ROWS][:, 0:1],
                buffer[k, FINE_ROWS : FINE_ROWS + 1],
                buffer[k, 0:FINE_ROWS][:, 1:2],
                buffer[k, FINE_ROWS + 1 : FINE_ROWS + 2],
            )

        def pick_lane(tall, index):
            lane = iota(tall.shape, 1)
            return jnp.sum(jnp.where(lane == index, tall, 0.0), axis=1, keepdims=True)

        def pick_row(wide, index):
            sub = iota(wide.shape, 0)
            return jnp.sum(jnp.where(sub == index, wide, 0.0), axis=0, keepdims=True)

        def next_sides(k):
            ring = ring_now[homes[k]]
            tall, wide = dot(grow, ring), dot(ring, spread[k])
            base = bands[k] * (LEFT + (RR - 1) * PW) + 3 * columns[k]
            level_w, flux_w, level_e = [pick_lane(tall, base + i) for i in range(3)]
            level_n, flux_n, level_s = [pick_row(wide, 3 * bands[k] + i) for i in range(3)]
            flux_line = pick_row(ring, 3 * bands[k] + 1)
            first = LEFT + columns[k] * PW
            own = dot(dot(grow, ret_now[k]), widen)
            surface, eastward, southward = [own[:, f * width : (f + 1) * width] for f in range(3)]
            depth_w, depth_n, open_w, open_n = kept(fixed_terms, k)

            taken = []
            for device, slot, cover in near[k]:
                edges = edge_now[device]
                chosen = edges
                for other in range(1, K):
                    chosen = jnp.where(
                        jnp.full(edges.shape, slot, jnp.int32) == other,
                        pltpu.roll(edges, width - 8 * other, 1),
                        chosen,
                    )
                taken.append((dot(grow, chosen), jnp.full((FINE_ROWS, 1), cover, jnp.int32) > 0))
            (left, has_left), (right, has_right) = taken
            s_l, e_l, e_p, q_l = [left[:, i : i + 1] for i in range(4)]
            s_f, e_f, q_f = [right[:, i : i + 1] for i in range(4, 7)]
            left_level = s_l - COURANT * ((e_l - e_p) + (q_l - below(q_l, pick_lane(flux_line, first - 1))))
            right_level = s_f - COURANT * (e_f + (q_f - below(q_f, pick_lane(flux_line, first + PW))))
            level_w = jnp.where(has_left, left_level, level_w)
            flux_w = jnp.where(has_left, e_l, flux_w)
            level_e = jnp.where(has_right, right_level, level_e)

            cols, rows = iota((FINE_ROWS, width), 1), iota((FINE_ROWS, width), 0)
            behind = jnp.where(cols < RR, flux_w, pltpu.roll(eastward, RR, 1))
            above = jnp.where(rows < RR, flux_n, pltpu.roll(southward, RR, 0))
            level = surface - COURANT * ((eastward - behind) + (southward - above))
            west_cell = level[:, 0:1]
            north_cell = level[0:1, :]
            west = open_w * (
                flux_w - COURANT * (depth_w + 0.5 * (level_w + west_cell)) * (west_cell - level_w)
            )
            north = open_n * (
                flux_n - COURANT * (depth_n + 0.5 * (level_n + north_cell)) * (north_cell - level_n)
            )
            east = level_e + COURANT * eastward[:, width - 1 : width]
            south = level_s + COURANT * southward[FINE_ROWS - 1 : FINE_ROWS, :]
            return west, north, east, south

        def below(column, top):
            wide = jnp.broadcast_to(column, (FINE_ROWS, width))
            rows = iota((FINE_ROWS, width), 0)
            return jnp.where(rows < RR, top, pltpu.roll(wide, RR, 0))[:, 0:1]

        pl.semaphore_wait(barrier, 2 * tiles - 1)
        wait_all(first_in, first_sems.at[1])
        for k in range(K):
            keep(ghosts.at[0], k, side_ghosts(first_in[homes[k], 0], k))
            keep(ghosts.at[1], k, side_ghosts(first_in[homes[k], 1], k))

        @pl.loop(0, STEPS)
        def _(s):
            edge = jnp.zeros((PH, width), jnp.float32)
            lane = iota((PH, width), 1)
            for k in range(K):
                slot = pl.ds(k * FINE_ROWS, FINE_ROWS)
                old, new = kept(ghosts.at[0], k), kept(ghosts.at[1], k)
                surface, eastward, southward = st[0, slot], st[1, slot], st[2, slot]
                depth = [depth_ref[0, i, slot] for i in range(2)]
                opened = [open_ref[0, i, slot].astype(jnp.float32) for i in range(2)]
                for m in range(1, RR + 1):
                    west_g, north_g, east_g, south_g = [
                        a + (m / RR) * (b - a) for a, b in zip(old, new)
                    ]
                    surface = new_level(surface, eastward, southward, west_g, north_g)
                    eastward, southward = new_fluxes(
                        eastward, southward, surface, east_g, south_g, depth, opened
                    )
                st[0, slot] = surface
                st[1, slot] = eastward
                st[2, slot] = southward
                packed = dot(jnp.concatenate([surface, eastward, southward], axis=1), gather)
                both = dot(shrink, packed)
                mean = lane < 2 * PW
                for i, (f, c) in enumerate(EDGES):
                    if f < 2:
                        mean = mean | (lane == 3 * PW + i)
                both = jnp.where(mean, both[0:PH], both[PH : 2 * PH])
                ret_out[s, k] = both
                ret_now[k] = both
                shifted = pltpu.roll(both, (8 * k - 3 * PW) % width, 1)
                edge = jnp.where((lane >= 8 * k) & (lane < 8 * k + 8), shifted, edge)

            @pl.when(s < STEPS - 1)
            def _():
                edge_out[s] = edge
                send_to(1, tiles - 1, edge_out.at[s], edge_in.at[s, tile], edge_send.at[s], edge_recv.at[s])

            send_all(ret_out.at[s], ret_in.at[s, pl.ds(tile * K, K)], ret_send.at[s], ret_recv.at[s])

            @pl.when(s == 0)
            def _():
                wait_all(fixed_in, fixed_sems.at[1])
                for k in range(K):
                    fixed = fixed_in[homes[k]]
                    tall, wide = dot(grow, fixed), dot(fixed, spread[k])
                    base = bands[k] * (LEFT + (RR - 1) * PW) + 3 * columns[k]
                    keep(
                        fixed_terms,
                        k,
                        (
                            pick_lane(tall, base),
                            pick_row(wide, 3 * bands[k]),
                            pick_lane(tall, base + 1),
                            pick_row(wide, 3 * bands[k] + 1),
                        ),
                    )

            @pl.when(s < STEPS - 1)
            def _():
                wait_all(ring_in.at[s], ring_recv.at[s])
                ring_now[...] = ring_in[s]
                wait_all(edge_in.at[s, pl.ds(0, tiles - 1)], edge_recv.at[s])
                edge_now[...] = edge_in[s]
                edge_now[tile] = edge
                for k in range(K):
                    ghosts[0, k] = ghosts[1, k]
                    keep(ghosts.at[1], k, next_sides(k))

        for k in range(K):
            slot = pl.ds(k * FINE_ROWS, FINE_ROWS)
            live = jnp.full((FINE_ROWS, width), lives[k], jnp.int32) > 0
            for f in range(3):
                out_ref[0, f, slot] = jnp.where(live, st[f, slot], state_ref[0, f, slot])

        for s in range(STEPS):
            wait_all(ret_in.at[s], ret_send.at[s])
        for s in range(STEPS - 1):
            wait_all(edge_in.at[s, pl.ds(0, tiles - 1)], edge_send.at[s])


def on_device(n_row, n_nest, ocean_state, face_depth, face_open, nest_place, nest_host):
    tiles = n_row * n_nest
    height, width = ocean_state.shape[2:]
    f32 = jnp.float32
    vmem = pl.BlockSpec(memory_space=pltpu.VMEM)
    smem = pl.BlockSpec(memory_space=pltpu.SMEM)
    dma = pltpu.SemaphoreType.DMA
    return pl.pallas_call(
        functools.partial(kernel, n_row, n_nest),
        out_shape=jax.ShapeDtypeStruct(ocean_state.shape, f32),
        in_specs=[smem, smem, vmem, vmem, vmem],
        out_specs=vmem,
        scratch_shapes=[
            pltpu.VMEM((3, height, width), f32),
            pltpu.VMEM((6, height, width), f32),
            pltpu.VMEM((2, PH, width), f32),
            pltpu.VMEM((tiles, 2, PH, width), f32),
            pltpu.VMEM((PH, width), f32),
            pltpu.VMEM((tiles, PH, width), f32),
            pltpu.VMEM((STEPS - 1, PH, width), f32),
            pltpu.VMEM((STEPS - 1, tiles, PH, width), f32),
            pltpu.VMEM((STEPS - 1, PH, width), f32),
            pltpu.VMEM((STEPS - 1, tiles, PH, width), f32),
            pltpu.VMEM((STEPS, K, PH, width), f32),
            pltpu.VMEM((STEPS, tiles * K, PH, width), f32),
            pltpu.VMEM((STEPS, height, width), f32),
            pltpu.VMEM((STEPS, 8, width), f32),
            pltpu.VMEM((STEPS, height, width), f32),
            pltpu.VMEM((STEPS, height, width), f32),
            pltpu.VMEM((STEPS, 8, width), f32),
            pltpu.VMEM((STEPS, height, width), f32),
            pltpu.VMEM((STEPS, 8, width), f32),
            pltpu.VMEM((K, width, width), f32),
            pltpu.VMEM((2, K, FINE_ROWS + 8, width), f32),
            pltpu.VMEM((tiles, PH, width), f32),
            pltpu.VMEM((tiles, PH, width), f32),
            pltpu.VMEM((tiles * K, PH, width), f32),
            pltpu.VMEM((K, FINE_ROWS + 8, width), f32),
            dma((2,)),
            dma((2,)),
            dma((STEPS - 1,)),
            dma((STEPS - 1,)),
            dma((STEPS - 1,)),
            dma((STEPS - 1,)),
            dma((STEPS,)),
            dma((STEPS,)),
            dma((STEPS, 4)),
            dma((STEPS, 4)),
        ],
        compiler_params=pltpu.CompilerParams(collective_id=0, has_side_effects=True),
    )(nest_place, nest_host, ocean_state, face_depth, face_open)


def solution(mesh):
    field = P("sec", None, "row", "nest")
    return jax.shard_map(
        functools.partial(on_device, mesh.shape["row"], mesh.shape["nest"]),
        mesh=mesh,
        in_specs=(field, field, field, P(), P()),
        out_specs=field,
        check_vma=False,
    )
```

```python
import functools

import jax
import jax.numpy as jnp
from jax import lax
from jax.experimental import pallas as pl
from jax.experimental.pallas import tpu as pltpu
from jax.sharding import PartitionSpec as P

PH = 8
PW = 32
RR = 4
K = 2
STEPS = 4
NPOS = K * (RR - 1)
COURANT = 0.3
HIGHEST = lax.Precision.HIGHEST
MESH = pl.DeviceIdType.MESH
FINE_ROWS = RR * PH
TOP = (RR - 1) * PH // 2
LEFT = PW // 2
EDGES = ((0, PW - 1), (1, PW - 1), (1, PW - 2), (2, PW - 1), (0, 0), (1, 0), (2, 0))


def iota(shape, dim):
    return lax.broadcasted_iota(jnp.int32, shape, dim)


def new_level(surface, eastward, southward, west_ghost, north_ghost):
    rows, cols = iota(surface.shape, 0), iota(surface.shape, 1)
    east_behind = jnp.where(cols == 0, west_ghost, pltpu.roll(eastward, 1, 1))
    south_behind = jnp.where(rows == 0, north_ghost, pltpu.roll(southward, 1, 0))
    return surface - COURANT * ((eastward - east_behind) + (southward - south_behind))


def new_fluxes(eastward, southward, level, east_ghost, south_ghost, depth, opened):
    height, width = level.shape
    rows, cols = iota(level.shape, 0), iota(level.shape, 1)
    level_east = jnp.where(cols == width - 1, east_ghost, pltpu.roll(level, width - 1, 1))
    level_south = jnp.where(rows == height - 1, south_ghost, pltpu.roll(level, height - 1, 0))
    east = opened[0] * (
        eastward - COURANT * (depth[0] + 0.5 * (level + level_east)) * (level_east - level)
    )
    south = opened[1] * (
        southward - COURANT * (depth[1] + 0.5 * (level + level_south)) * (level_south - level)
    )
    return east, south


def dot(a, b):
    return jnp.dot(a, b, precision=HIGHEST, preferred_element_type=jnp.float32)


def pack_strips(tmp):
    width = tmp.shape[2]
    lane, sub = iota((PH, width), 1), iota((PH, width), 0)
    block = jnp.zeros((PH, width), jnp.float32)
    span = (RR - 1) * PW
    inner = (lane >= LEFT) & (lane < LEFT + span)
    for band in range(K):
        first = band * FINE_ROWS + TOP
        east8 = tmp[1, first : first + PH, :]
        level8 = tmp[0, first : first + PH, :]
        for j in range(RR - 1):
            column = LEFT + j * PW
            west_lane = band * 2 * (RR - 1) + j
            east_lane = west_lane + RR - 1
            block = jnp.where(
                lane == west_lane, pltpu.roll(east8, (west_lane - column + 1) % width, 1), block
            )
            block = jnp.where(
                lane == east_lane, pltpu.roll(level8, (east_lane - column - PW) % width, 1), block
            )
        block = jnp.where(inner & (sub == 2 * band), tmp[2, first - 1 : first, :], block)
        block = jnp.where(inner & (sub == 2 * band + 1), tmp[0, first + PH : first + PH + 1, :], block)
    return block


def pack_ring(sides, lines):
    ref, width = sides[0][0], sides[0][0].shape[-1]
    lane, sub = iota((PH, width), 1), iota((PH, width), 0)
    span = (RR - 1) * PW
    block = jnp.zeros((PH, width), jnp.float32)
    inner = (lane >= LEFT) & (lane < LEFT + span)
    for band in range(K):
        first = band * FINE_ROWS + TOP
        base = band * (LEFT + span)
        for i, (ref, index, shift) in enumerate(sides):
            values = ref[index + (slice(first, first + PH), slice(None))].astype(jnp.float32)
            for j in range(RR - 1):
                target = base + 3 * j + i
                source = LEFT + j * PW + shift
                block = jnp.where(
                    lane == target, pltpu.roll(values, (target - source) % width, 1), block
                )
        for i, (ref, index, shift) in enumerate(lines):
            at = first + shift
            line = ref[index + (slice(at, at + 1), slice(None))].astype(jnp.float32)
            block = jnp.where(inner & (sub == 3 * band + i), line, block)
    return block


def kernel(
    n_row,
    n_nest,
    place_ref,
    host_ref,
    state_ref,
    depth_ref,
    open_ref,
    out_ref,
    st,
    tmp,
    first_out,
    first_in,
    fixed_out,
    fixed_in,
    ring_out,
    ring_in,
    edge_out,
    edge_in,
    ret_out,
    ret_in,
    east_out,
    south_out,
    level_out,
    west_in,
    north_in,
    east_in,
    south_in,
    spread,
    ghosts,
    ring_now,
    edge_now,
    ret_now,
    fixed_terms,
    first_sems,
    fixed_sems,
    ring_send,
    ring_recv,
    edge_send,
    edge_recv,
    ret_send,
    ret_recv,
    halo_send,
    halo_recv,
):
    tiles = n_row * n_nest
    nests = place_ref.shape[0]
    sec, row, col = lax.axis_index("sec"), lax.axis_index("row"), lax.axis_index("nest")
    tile = row * n_nest + col
    is_outer = sec == 0
    has_west, has_east = col > 0, col < n_nest - 1
    has_north, has_south = row > 0, row < n_row - 1
    west, east = (sec, row, col - 1), (sec, row, col + 1)
    north, south = (sec, row - 1, col), (sec, row + 1, col)
    links = ((has_west, west), (has_east, east), (has_north, north), (has_south, south))
    height, width = state_ref.shape[2], state_ref.shape[3]

    barrier = pltpu.get_barrier_semaphore()

    @pl.loop(0, tiles)
    def _(i):
        t = lax.rem(tile + i, tiles)
        pl.semaphore_signal(
            barrier, inc=1, device_id=(1 - sec, t // n_nest, lax.rem(t, n_nest)), device_id_type=MESH
        )

    def send_to(section, count, src, dst, send_sem, recv_sem):
        @pl.loop(0, tiles)
        def _(i):
            t = lax.rem(2 * tiles - 1 - tile - i, tiles)

            def go():
                pltpu.make_async_remote_copy(
                    src_ref=src,
                    dst_ref=dst,
                    send_sem=send_sem,
                    recv_sem=recv_sem,
                    device_id=(section, t // n_nest, lax.rem(t, n_nest)),
                    device_id_type=MESH,
                ).start()

            if count == tiles:
                go()
            else:
                pl.when(t != tile)(go)

    def send_all(src, dst, send_sem, recv_sem):
        send_to(1 - sec, tiles, src, dst, send_sem, recv_sem)

    def wait_all(whole, sem):
        pltpu.make_async_copy(whole, whole, sem).wait()

    @pl.when(is_outer)
    def _():
        for present, device in links:

            @pl.when(present)
            def _():
                pl.semaphore_signal(barrier, inc=1, device_id=device, device_id_type=MESH)

        st[...] = state_ref[0]
        depth = [depth_ref[0, i] for i in range(2)]
        opened = [open_ref[0, i].astype(jnp.float32) for i in range(2)]
        slots, covers = [], []
        for p in range(NPOS):
            slot, cover = jnp.int32(0), jnp.int32(0)
            for n in range(nests):
                hit = place_ref[n] == tile * NPOS + p
                slot = jnp.where(hit, host_ref[n], slot)
                cover = jnp.where(hit, 1, cover)
            slots.append(slot)
            covers.append(cover)
        zero_block = jnp.zeros((height, width), jnp.float32)
        for present, buffer in (
            (has_west, west_in),
            (has_east, east_in),
            (has_north, north_in),
            (has_south, south_in),
        ):

            @pl.when(jnp.logical_not(present))
            def _():
                for s in range(STEPS):
                    buffer[s] = jnp.zeros(buffer.shape[1:], jnp.float32)

        def halo(s, kind, src, dst, device):
            return pltpu.make_async_remote_copy(
                src_ref=src,
                dst_ref=dst,
                send_sem=halo_send.at[s, kind],
                recv_sem=halo_recv.at[s, kind],
                device_id=device,
                device_id_type=MESH,
            )

        @pl.loop(0, STEPS)
        def _(s):
            surface, eastward, southward = st[0], st[1], st[2]
            level = new_level(surface, eastward, southward, 0.0, 0.0)
            fluxes = new_fluxes(eastward, southward, level, 0.0, 0.0, depth, opened)
            tmp[0] = level
            tmp[1] = fluxes[0]
            tmp[2] = fluxes[1]

            @pl.when(s == 0)
            def _():
                first_out[0] = pack_strips(st)
                first_out[1] = pack_strips(tmp)
                peers = jnp.int32(tiles)
                for present, _device in links:
                    peers = peers + jnp.where(present, 1, 0)
                pl.semaphore_wait(barrier, peers)
                send_all(first_out, first_in.at[tile], first_sems.at[0], first_sems.at[1])

            @pl.when(s < STEPS - 1)
            def _():
                cols = iota((height, width), 1)
                rows = iota((height, width), 0)
                east_gap = fluxes[0] - jnp.where(cols == 0, 0.0, pltpu.roll(fluxes[0], 1, 1))
                south_gap = fluxes[1] - jnp.where(rows == 0, 0.0, pltpu.roll(fluxes[1], 1, 0))
                tmp[3] = level - COURANT * (east_gap + south_gap)
                tmp[4] = level - COURANT * (fluxes[0] + south_gap)
                tmp[5] = level - COURANT * (east_gap + fluxes[1])
                ring_out[s] = pack_ring(
                    [(tmp, (3,), -1), (tmp, (1,), -1), (tmp, (4,), PW)],
                    [(tmp, (3,), -1), (tmp, (2,), -1), (tmp, (5,), PH)],
                )
                send_all(ring_out.at[s], ring_in.at[s, tile], ring_send.at[s], ring_recv.at[s])

            @pl.when(s == 0)
            def _():
                fixed_out[...] = pack_ring(
                    [(depth_ref, (0, 0), -1), (open_ref, (0, 0), -1)],
                    [(depth_ref, (0, 1), -1), (open_ref, (0, 1), -1)],
                )
                send_all(fixed_out, fixed_in.at[tile], fixed_sems.at[0], fixed_sems.at[1])

            east_out[s] = eastward
            south_out[s] = southward[height - 8 :]
            to_east = halo(s, 0, east_out.at[s], west_in.at[s], east)
            to_south = halo(s, 1, south_out.at[s], north_in.at[s], south)
            to_west = halo(s, 2, level_out.at[s], east_in.at[s], west)
            to_north = halo(s, 3, level_out.at[s, pl.ds(0, 8)], south_in.at[s], north)

            @pl.when(has_east)
            def _():
                to_east.start()

            @pl.when(has_south)
            def _():
                to_south.start()

            @pl.when(has_west)
            def _():
                to_east.wait_recv()

            @pl.when(has_north)
            def _():
                to_south.wait_recv()

            level = new_level(
                surface,
                eastward,
                southward,
                west_in[s][:, width - 1 : width],
                north_in[s][7:8, :],
            )
            level_out[s] = level

            @pl.when(has_west)
            def _():
                to_west.start()

            @pl.when(has_north)
            def _():
                to_north.start()

            @pl.when(has_east)
            def _():
                to_west.wait_recv()

            @pl.when(has_south)
            def _():
                to_north.wait_recv()

            fluxes = new_fluxes(
                eastward, southward, level, east_in[s][:, 0:1], south_in[s][0:1, :], depth, opened
            )
            st[0] = level
            st[1] = fluxes[0]
            st[2] = fluxes[1]

            wait_all(ret_in.at[s], ret_recv.at[s])
            ret_now[...] = ret_in[s]
            lane = iota((PH, width), 1)
            for band in range(K):
                first = band * FINE_ROWS + TOP
                merged = [st[f, first : first + PH, :] for f in range(3)]
                for j in range(RR - 1):
                    p = band * (RR - 1) + j
                    column = LEFT + j * PW
                    block = ret_now[slots[p]]
                    mask = (
                        (lane >= column)
                        & (lane < column + PW)
                        & (jnp.full((PH, width), covers[p], jnp.int32) > 0)
                    )
                    for f in range(3):
                        shifted = pltpu.roll(block, (column - f * PW) % width, 1)
                        merged[f] = jnp.where(mask, shifted, merged[f])
                for f in range(3):
                    st[f, first : first + PH, :] = merged[f]

        out_ref[0] = st[...]

        for s in range(STEPS):

            @pl.when(has_east)
            def _():
                halo(s, 0, east_out.at[s], west_in.at[s], east).wait_send()

            @pl.when(has_south)
            def _():
                halo(s, 1, south_out.at[s], north_in.at[s], south).wait_send()

            @pl.when(has_west)
            def _():
                halo(s, 2, level_out.at[s], east_in.at[s], west).wait_send()

            @pl.when(has_north)
            def _():
                halo(s, 3, level_out.at[s, pl.ds(0, 8)], south_in.at[s], north).wait_send()

        wait_all(first_in, first_sems.at[0])
        wait_all(fixed_in, fixed_sems.at[0])
        for s in range(STEPS - 1):
            wait_all(ring_in.at[s], ring_send.at[s])

    @pl.when(jnp.logical_not(is_outer))
    def _():
        @pl.loop(0, tiles - 1)
        def _(i):
            t = lax.rem(tile + i + 1, tiles)
            pl.semaphore_signal(
                barrier, inc=1, device_id=(sec, t // n_nest, lax.rem(t, n_nest)), device_id_type=MESH
            )

        st[...] = state_ref[0]
        spots, lives = [], []
        for k in range(K):
            spot, live = jnp.int32(0), jnp.int32(0)
            for n in range(nests):
                hit = host_ref[n] == tile * K + k
                spot = jnp.where(hit, place_ref[n], spot)
                live = jnp.where(hit, 1, live)
            spots.append(spot)
            lives.append(live)
        homes = [spot // NPOS for spot in spots]
        bands = [lax.rem(spot, NPOS) // (RR - 1) for spot in spots]
        columns = [lax.rem(spot, RR - 1) for spot in spots]
        near = []
        for k in range(K):
            pair = []
            for side in (-1, 1):
                inside = (columns[k] + side >= 0) & (columns[k] + side < RR - 1)
                slot, cover = jnp.int32(0), jnp.int32(0)
                for n in range(nests):
                    hit = inside & (place_ref[n] == spots[k] + side)
                    slot = jnp.where(hit, host_ref[n], slot)
                    cover = jnp.where(hit, 1, cover)
                pair.append((slot // K, lax.rem(slot, K), cover))
            near.append(pair)
        for k in range(K):
            source = iota((width, width), 0)
            fine = iota((width, width), 1)
            wanted = LEFT + columns[k] * PW + fine // RR
            spread[k] = (source == wanted).astype(jnp.float32)
        grow = (iota((FINE_ROWS, PH), 0) // RR == iota((FINE_ROWS, PH), 1)).astype(jnp.float32)
        gather_from = iota((3 * width, 2 * width), 0)
        gather_to = iota((3 * width, 2 * width), 1)
        field, lane_in = gather_from // width, lax.rem(gather_from, width)
        weight = jnp.where(
            field == 1, jnp.where(lax.rem(lane_in, RR) == RR - 1, 1.0, 0.0), 1.0 / RR
        )
        gather = jnp.where(gather_to == field * PW + lane_in // RR, weight, 0.0)
        for i, (f, c) in enumerate(EDGES):
            gather = gather + jnp.where(
                (gather_to >= width)
                & (lax.rem(gather_to, 8 * K) == i)
                & (field == f)
                & (lane_in // RR == c),
                weight,
                0.0,
            )
        fold_to = iota((width, width), 1)
        fold = (
            (lax.rem(iota((width, width), 0), 8 * K) == fold_to) & (fold_to < 8 * K)
        ).astype(jnp.float32)
        widen_to = iota((width, 3 * width), 1)
        widen = (
            iota((width, 3 * width), 0)
            == (widen_to // width) * PW + lax.rem(widen_to, width) // RR
        ).astype(jnp.float32)
        shrink_row = iota((2 * PH, FINE_ROWS), 0)
        shrink_from = iota((2 * PH, FINE_ROWS), 1)
        shrink = jnp.where(
            shrink_row < PH,
            jnp.where(shrink_from // RR == shrink_row, 1.0 / RR, 0.0),
            jnp.where(shrink_from == (shrink_row - PH) * RR + RR - 1, 1.0, 0.0),
        )

        def side_ghosts(block, k):
            lane, sub = iota((PH, width), 1), iota((PH, width), 0)
            tall_lane = iota((FINE_ROWS, width), 1)
            tall = dot(grow, block)
            wide = dot(block, spread[k])
            west_lane = bands[k] * (2 * (RR - 1)) + columns[k]
            west = jnp.sum(jnp.where(tall_lane == west_lane, tall, 0.0), axis=1, keepdims=True)
            east = jnp.sum(
                jnp.where(tall_lane == west_lane + (RR - 1), tall, 0.0), axis=1, keepdims=True
            )
            north = jnp.sum(jnp.where(sub == 2 * bands[k], wide, 0.0), axis=0, keepdims=True)
            south = jnp.sum(jnp.where(sub == 2 * bands[k] + 1, wide, 0.0), axis=0, keepdims=True)
            return west, north, east, south

        def keep(buffer, k, sides):
            west, north, east, south = sides
            lane = iota((FINE_ROWS, width), 1)
            buffer[k, 0:FINE_ROWS] = jnp.where(lane == 0, west, east)
            buffer[k, FINE_ROWS : FINE_ROWS + 8] = jnp.where(
                iota((8, width), 0) == 0, north, south
            )

        def kept(buffer, k):
            return (
                buffer[k, 0:FINE_ROWS][:, 0:1],
                buffer[k, FINE_ROWS : FINE_ROWS + 1],
                buffer[k, 0:FINE_ROWS][:, 1:2],
                buffer[k, FINE_ROWS + 1 : FINE_ROWS + 2],
            )

        def pick_lane(tall, index):
            lane = iota(tall.shape, 1)
            return jnp.sum(jnp.where(lane == index, tall, 0.0), axis=1, keepdims=True)

        def pick_row(wide, index):
            sub = iota(wide.shape, 0)
            return jnp.sum(jnp.where(sub == index, wide, 0.0), axis=0, keepdims=True)

        def ring_terms(k):
            ring = ring_now[homes[k]]
            tall, wide = dot(grow, ring), dot(ring, spread[k])
            base = bands[k] * (LEFT + (RR - 1) * PW) + 3 * columns[k]
            sides = [pick_lane(tall, base + i) for i in range(3)]
            lines = [pick_row(wide, 3 * bands[k] + i) for i in range(3)]
            flux_line = pick_row(ring, 3 * bands[k] + 1)
            first = LEFT + columns[k] * PW
            corners = [pick_lane(flux_line, first - 1), pick_lane(flux_line, first + PW)]
            return sides, lines, corners

        def next_sides(k, own, ring):
            (level_w, flux_w, level_e), (level_n, flux_n, level_s), (corner_w, corner_e) = ring
            surface, eastward, southward = [own[:, f * width : (f + 1) * width] for f in range(3)]
            depth_w, depth_n, open_w, open_n = kept(fixed_terms, k)

            taken = []
            for device, slot, cover in near[k]:
                line = jnp.broadcast_to(edge_now[device, 0:1], (FINE_ROWS, width))
                own_row = iota((FINE_ROWS, width), 1) // (8 * K) == iota((FINE_ROWS, width), 0) // RR
                edges = dot(jnp.where(own_row, line, 0.0), fold)
                chosen = edges
                for other in range(1, K):
                    chosen = jnp.where(
                        jnp.full(edges.shape, slot, jnp.int32) == other,
                        pltpu.roll(edges, width - 8 * other, 1),
                        chosen,
                    )
                taken.append((chosen, jnp.full((FINE_ROWS, 1), cover, jnp.int32) > 0))
            (left, has_left), (right, has_right) = taken
            s_l, e_l, e_p, q_l = [left[:, i : i + 1] for i in range(4)]
            s_f, e_f, q_f = [right[:, i : i + 1] for i in range(4, 7)]
            left_level = s_l - COURANT * ((e_l - e_p) + (q_l - below(q_l, corner_w)))
            right_level = s_f - COURANT * (e_f + (q_f - below(q_f, corner_e)))
            level_w = jnp.where(has_left, left_level, level_w)
            flux_w = jnp.where(has_left, e_l, flux_w)
            level_e = jnp.where(has_right, right_level, level_e)

            cols, rows = iota((FINE_ROWS, width), 1), iota((FINE_ROWS, width), 0)
            behind = jnp.where(cols < RR, flux_w, pltpu.roll(eastward, RR, 1))
            above = jnp.where(rows < RR, flux_n, pltpu.roll(southward, RR, 0))
            level = surface - COURANT * ((eastward - behind) + (southward - above))
            west_cell = level[:, 0:1]
            north_cell = level[0:1, :]
            west = open_w * (
                flux_w - COURANT * (depth_w + 0.5 * (level_w + west_cell)) * (west_cell - level_w)
            )
            north = open_n * (
                flux_n - COURANT * (depth_n + 0.5 * (level_n + north_cell)) * (north_cell - level_n)
            )
            east = level_e + COURANT * eastward[:, width - 1 : width]
            south = level_s + COURANT * southward[FINE_ROWS - 1 : FINE_ROWS, :]
            return west, north, east, south

        def below(column, top):
            wide = jnp.broadcast_to(column, (FINE_ROWS, width))
            rows = iota((FINE_ROWS, width), 0)
            return jnp.where(rows < RR, top, pltpu.roll(wide, RR, 0))[:, 0:1]

        pl.semaphore_wait(barrier, 2 * tiles - 1)
        wait_all(first_in, first_sems.at[1])
        for k in range(K):
            keep(ghosts.at[0], k, side_ghosts(first_in[homes[k], 0], k))
            keep(ghosts.at[1], k, side_ghosts(first_in[homes[k], 1], k))

        @pl.loop(0, STEPS)
        def _(s):
            edge = jnp.zeros((PH, width), jnp.float32)
            lane = iota((PH, width), 1)
            for k in range(K):
                slot = pl.ds(k * FINE_ROWS, FINE_ROWS)
                old, new = kept(ghosts.at[0], k), kept(ghosts.at[1], k)
                surface, eastward, southward = st[0, slot], st[1, slot], st[2, slot]
                depth = [depth_ref[0, i, slot] for i in range(2)]
                opened = [open_ref[0, i, slot].astype(jnp.float32) for i in range(2)]
                for m in range(1, RR + 1):
                    west_g, north_g, east_g, south_g = [
                        a + (m / RR) * (b - a) for a, b in zip(old, new)
                    ]
                    surface = new_level(surface, eastward, southward, west_g, north_g)
                    eastward, southward = new_fluxes(
                        eastward, southward, surface, east_g, south_g, depth, opened
                    )
                st[0, slot] = surface
                st[1, slot] = eastward
                st[2, slot] = southward
                packed = dot(jnp.concatenate([surface, eastward, southward], axis=1), gather)
                both = dot(shrink, packed)
                block = jnp.where(
                    lane < 2 * PW, both[0:PH, 0:width], both[PH : 2 * PH, 0:width]
                )
                ret_out[s, k] = block
                ret_now[k] = block
                spot = lax.rem(lane, 8 * K)
                mean = spot < 0
                for i, (f, c) in enumerate(EDGES):
                    if f < 2:
                        mean = mean | (spot == i)
                side = jnp.where(mean, both[0:PH, width:], both[PH : 2 * PH, width:])
                side = jnp.where(lane // (8 * K) == iota((PH, width), 0), side, 0.0)
                edge = edge + pltpu.roll(side, 8 * k, 1)

            @pl.when(s < STEPS - 1)
            def _():
                edge_out[s, 0:1] = jnp.sum(edge, axis=0, keepdims=True)
                send_to(
                    1,
                    tiles - 1,
                    edge_out.at[s, pl.ds(0, 1)],
                    edge_in.at[s, tile, pl.ds(0, 1)],
                    edge_send.at[s],
                    edge_recv.at[s],
                )

            send_all(ret_out.at[s], ret_in.at[s, pl.ds(tile * K, K)], ret_send.at[s], ret_recv.at[s])

            @pl.when(s == 0)
            def _():
                wait_all(fixed_in, fixed_sems.at[1])
                for k in range(K):
                    fixed = fixed_in[homes[k]]
                    tall, wide = dot(grow, fixed), dot(fixed, spread[k])
                    base = bands[k] * (LEFT + (RR - 1) * PW) + 3 * columns[k]
                    keep(
                        fixed_terms,
                        k,
                        (
                            pick_lane(tall, base),
                            pick_row(wide, 3 * bands[k]),
                            pick_lane(tall, base + 1),
                            pick_row(wide, 3 * bands[k] + 1),
                        ),
                    )

            @pl.when(s < STEPS - 1)
            def _():
                owns = []
                for k in range(K):
                    ghosts[0, k] = ghosts[1, k]
                    owns.append(dot(dot(grow, ret_now[k]), widen))
                wait_all(ring_in.at[s], ring_recv.at[s])
                ring_now[...] = ring_in[s]
                rings = [ring_terms(k) for k in range(K)]
                wait_all(edge_in.at[s, pl.ds(0, tiles - 1), pl.ds(0, 1)], edge_recv.at[s])
                edge_now[:, 0:1] = edge_in[s, :, 0:1]
                edge_now[tile, 0:1] = edge_out[s, 0:1]
                for k in range(K):
                    keep(ghosts.at[1], k, next_sides(k, owns[k], rings[k]))

        for k in range(K):
            slot = pl.ds(k * FINE_ROWS, FINE_ROWS)
            live = jnp.full((FINE_ROWS, width), lives[k], jnp.int32) > 0
            for f in range(3):
                out_ref[0, f, slot] = jnp.where(live, st[f, slot], state_ref[0, f, slot])

        for s in range(STEPS):
            wait_all(ret_in.at[s], ret_send.at[s])
        for s in range(STEPS - 1):
            wait_all(edge_in.at[s, pl.ds(0, tiles - 1), pl.ds(0, 1)], edge_send.at[s])


def on_device(n_row, n_nest, ocean_state, face_depth, face_open, nest_place, nest_host):
    tiles = n_row * n_nest
    height, width = ocean_state.shape[2:]
    f32 = jnp.float32
    vmem = pl.BlockSpec(memory_space=pltpu.VMEM)
    smem = pl.BlockSpec(memory_space=pltpu.SMEM)
    dma = pltpu.SemaphoreType.DMA
    return pl.pallas_call(
        functools.partial(kernel, n_row, n_nest),
        out_shape=jax.ShapeDtypeStruct(ocean_state.shape, f32),
        in_specs=[smem, smem, vmem, vmem, vmem],
        out_specs=vmem,
        scratch_shapes=[
            pltpu.VMEM((3, height, width), f32),
            pltpu.VMEM((6, height, width), f32),
            pltpu.VMEM((2, PH, width), f32),
            pltpu.VMEM((tiles, 2, PH, width), f32),
            pltpu.VMEM((PH, width), f32),
            pltpu.VMEM((tiles, PH, width), f32),
            pltpu.VMEM((STEPS - 1, PH, width), f32),
            pltpu.VMEM((STEPS - 1, tiles, PH, width), f32),
            pltpu.VMEM((STEPS - 1, PH, width), f32),
            pltpu.VMEM((STEPS - 1, tiles, PH, width), f32),
            pltpu.VMEM((STEPS, K, PH, width), f32),
            pltpu.VMEM((STEPS, tiles * K, PH, width), f32),
            pltpu.VMEM((STEPS, height, width), f32),
            pltpu.VMEM((STEPS, 8, width), f32),
            pltpu.VMEM((STEPS, height, width), f32),
            pltpu.VMEM((STEPS, height, width), f32),
            pltpu.VMEM((STEPS, 8, width), f32),
            pltpu.VMEM((STEPS, height, width), f32),
            pltpu.VMEM((STEPS, 8, width), f32),
            pltpu.VMEM((K, width, width), f32),
            pltpu.VMEM((2, K, FINE_ROWS + 8, width), f32),
            pltpu.VMEM((tiles, PH, width), f32),
            pltpu.VMEM((tiles, PH, width), f32),
            pltpu.VMEM((tiles * K, PH, width), f32),
            pltpu.VMEM((K, FINE_ROWS + 8, width), f32),
            dma((2,)),
            dma((2,)),
            dma((STEPS - 1,)),
            dma((STEPS - 1,)),
            dma((STEPS - 1,)),
            dma((STEPS - 1,)),
            dma((STEPS,)),
            dma((STEPS,)),
            dma((STEPS, 4)),
            dma((STEPS, 4)),
        ],
        compiler_params=pltpu.CompilerParams(collective_id=0, has_side_effects=True),
    )(nest_place, nest_host, ocean_state, face_depth, face_open)


def solution(mesh):
    field = P("sec", None, "row", "nest")
    return jax.shard_map(
        functools.partial(on_device, mesh.shape["row"], mesh.shape["nest"]),
        mesh=mesh,
        in_specs=(field, field, field, P(), P()),
        out_specs=field,
        check_vma=False,
    )
```

```python
import functools

import jax
import jax.numpy as jnp
from jax import lax
from jax.experimental import pallas as pl
from jax.experimental.pallas import tpu as pltpu
from jax.sharding import PartitionSpec as P

PH = 8
PW = 32
RR = 4
K = 2
STEPS = 4
NPOS = K * (RR - 1)
COURANT = 0.3
MESH = pl.DeviceIdType.MESH
FINE_ROWS = RR * PH
TOP = (RR - 1) * PH // 2
LEFT = PW // 2
EDGES = ((0, PW - 1), (1, PW - 1), (1, PW - 2), (2, PW - 1), (0, 0), (1, 0), (2, 0))


def iota(shape, dim):
    return lax.broadcasted_iota(jnp.int32, shape, dim)


def new_level(surface, eastward, southward, west_ghost, north_ghost):
    rows, cols = iota(surface.shape, 0), iota(surface.shape, 1)
    east_behind = jnp.where(cols == 0, west_ghost, pltpu.roll(eastward, 1, 1))
    south_behind = jnp.where(rows == 0, north_ghost, pltpu.roll(southward, 1, 0))
    return surface - COURANT * ((eastward - east_behind) + (southward - south_behind))


def new_fluxes(eastward, southward, level, east_ghost, south_ghost, depth, opened):
    height, width = level.shape
    rows, cols = iota(level.shape, 0), iota(level.shape, 1)
    level_east = jnp.where(cols == width - 1, east_ghost, pltpu.roll(level, width - 1, 1))
    level_south = jnp.where(rows == height - 1, south_ghost, pltpu.roll(level, height - 1, 0))
    east = opened[0] * (
        eastward - COURANT * (depth[0] + 0.5 * (level + level_east)) * (level_east - level)
    )
    south = opened[1] * (
        southward - COURANT * (depth[1] + 0.5 * (level + level_south)) * (level_south - level)
    )
    return east, south


def parts(x):
    high = x.astype(jnp.bfloat16).astype(jnp.float32)
    rest = x - high
    middle = rest.astype(jnp.bfloat16).astype(jnp.float32)
    return high, middle, rest - middle


def dot_by(x, chosen):
    rows = x.shape[0]
    stacked = jnp.concatenate(parts(x), axis=0).astype(jnp.bfloat16)
    y = jnp.dot(stacked, chosen, preferred_element_type=jnp.float32)
    return y[:rows] + (y[rows : 2 * rows] + y[2 * rows :])


def dot_of(chosen, x):
    cols = x.shape[1]
    stacked = jnp.concatenate(parts(x), axis=1).astype(jnp.bfloat16)
    y = jnp.dot(chosen, stacked, preferred_element_type=jnp.float32)
    return y[:, :cols] + (y[:, cols : 2 * cols] + y[:, 2 * cols :])


def pack_strips(tmp):
    width = tmp.shape[2]
    lane, sub = iota((PH, width), 1), iota((PH, width), 0)
    block = jnp.zeros((PH, width), jnp.float32)
    span = (RR - 1) * PW
    inner = (lane >= LEFT) & (lane < LEFT + span)
    for band in range(K):
        first = band * FINE_ROWS + TOP
        east8 = tmp[1, first : first + PH, :]
        level8 = tmp[0, first : first + PH, :]
        for j in range(RR - 1):
            column = LEFT + j * PW
            west_lane = band * 2 * (RR - 1) + j
            east_lane = west_lane + RR - 1
            block = jnp.where(
                lane == west_lane, pltpu.roll(east8, (west_lane - column + 1) % width, 1), block
            )
            block = jnp.where(
                lane == east_lane, pltpu.roll(level8, (east_lane - column - PW) % width, 1), block
            )
        block = jnp.where(inner & (sub == 2 * band), tmp[2, first - 1 : first, :], block)
        block = jnp.where(inner & (sub == 2 * band + 1), tmp[0, first + PH : first + PH + 1, :], block)
    return block


def pack_ring(sides, lines):
    ref, width = sides[0][0], sides[0][0].shape[-1]
    lane, sub = iota((PH, width), 1), iota((PH, width), 0)
    span = (RR - 1) * PW
    block = jnp.zeros((PH, width), jnp.float32)
    inner = (lane >= LEFT) & (lane < LEFT + span)
    for band in range(K):
        first = band * FINE_ROWS + TOP
        base = band * (LEFT + span)
        for i, (ref, index, shift) in enumerate(sides):
            values = ref[index + (slice(first, first + PH), slice(None))].astype(jnp.float32)
            for j in range(RR - 1):
                target = base + 3 * j + i
                source = LEFT + j * PW + shift
                block = jnp.where(
                    lane == target, pltpu.roll(values, (target - source) % width, 1), block
                )
        for i, (ref, index, shift) in enumerate(lines):
            at = first + shift
            line = ref[index + (slice(at, at + 1), slice(None))].astype(jnp.float32)
            block = jnp.where(inner & (sub == 3 * band + i), line, block)
    return block


def fold_column(field, column):
    height, width = field.shape
    lane = iota((8, width), 1)
    block = jnp.zeros((8, width), jnp.float32)
    for v in range(height // 8):
        piece = pltpu.roll(field[8 * v : 8 * v + 8], (v - column) % width, 1)
        block = jnp.where(lane == v, piece, block)
    return block


def unfold_column(block, height):
    return jnp.concatenate([block[:, v : v + 1] for v in range(height // 8)], axis=0)


def kernel(
    n_row,
    n_nest,
    place_ref,
    host_ref,
    state_hbm,
    depth_hbm,
    open_hbm,
    out_ref,
    state_ref,
    depth_ref,
    open_ref,
    load_sems,
    st,
    tmp,
    first_out,
    first_in,
    fixed_out,
    fixed_in,
    ring_out,
    ring_in,
    edge_out,
    edge_in,
    ret_out,
    ret_in,
    east_out,
    south_out,
    level_out,
    west_out,
    west_in,
    north_in,
    east_in,
    south_in,
    spread,
    ghosts,
    ring_now,
    edge_now,
    ret_now,
    fixed_terms,
    first_sems,
    fixed_sems,
    ring_send,
    ring_recv,
    edge_send,
    edge_recv,
    ret_send,
    ret_recv,
    halo_send,
    halo_recv,
):
    tiles = n_row * n_nest
    nests = place_ref.shape[0]
    sec, row, col = lax.axis_index("sec"), lax.axis_index("row"), lax.axis_index("nest")
    tile = row * n_nest + col
    is_outer = sec == 0
    has_west, has_east = col > 0, col < n_nest - 1
    has_north, has_south = row > 0, row < n_row - 1
    west, east = (sec, row, col - 1), (sec, row, col + 1)
    north, south = (sec, row - 1, col), (sec, row + 1, col)
    links = ((has_west, west), (has_east, east), (has_north, north), (has_south, south))
    height, width = state_ref.shape[2], state_ref.shape[3]

    barrier = pltpu.get_barrier_semaphore()

    @pl.loop(0, tiles)
    def _(i):
        t = lax.rem(tile + i, tiles)
        pl.semaphore_signal(
            barrier, inc=1, device_id=(1 - sec, t // n_nest, lax.rem(t, n_nest)), device_id_type=MESH
        )

    loads = [
        pltpu.make_async_copy(source, target, load_sems.at[i])
        for i, (source, target) in enumerate(
            ((state_hbm, state_ref), (depth_hbm, depth_ref), (open_hbm, open_ref))
        )
    ]
    for load in loads:
        load.start()

    def send_to(section, count, src, dst, send_sem, recv_sem):
        @pl.loop(0, tiles)
        def _(i):
            t = lax.rem(2 * tiles - 1 - tile - i, tiles)

            def go():
                pltpu.make_async_remote_copy(
                    src_ref=src,
                    dst_ref=dst,
                    send_sem=send_sem,
                    recv_sem=recv_sem,
                    device_id=(section, t // n_nest, lax.rem(t, n_nest)),
                    device_id_type=MESH,
                ).start()

            if count == tiles:
                go()
            else:
                pl.when(t != tile)(go)

    def send_all(src, dst, send_sem, recv_sem):
        send_to(1 - sec, tiles, src, dst, send_sem, recv_sem)

    def wait_all(whole, sem):
        pltpu.make_async_copy(whole, whole, sem).wait()

    @pl.when(is_outer)
    def _():
        for present, device in links:

            @pl.when(present)
            def _():
                pl.semaphore_signal(barrier, inc=1, device_id=device, device_id_type=MESH)

        for load in loads:
            load.wait()
        st[...] = state_ref[0]
        depth = [depth_ref[0, i] for i in range(2)]
        opened = [open_ref[0, i].astype(jnp.float32) for i in range(2)]
        slots, covers = [], []
        for p in range(NPOS):
            slot, cover = jnp.int32(0), jnp.int32(0)
            for n in range(nests):
                hit = place_ref[n] == tile * NPOS + p
                slot = jnp.where(hit, host_ref[n], slot)
                cover = jnp.where(hit, 1, cover)
            slots.append(slot)
            covers.append(cover)
        zero_block = jnp.zeros((height, width), jnp.float32)
        for present, buffer in (
            (has_west, west_in),
            (has_east, east_in),
            (has_north, north_in),
            (has_south, south_in),
        ):

            @pl.when(jnp.logical_not(present))
            def _():
                for s in range(STEPS):
                    buffer[s] = jnp.zeros(buffer.shape[1:], jnp.float32)

        def halo(s, kind, src, dst, device):
            return pltpu.make_async_remote_copy(
                src_ref=src,
                dst_ref=dst,
                send_sem=halo_send.at[s, kind],
                recv_sem=halo_recv.at[s, kind],
                device_id=device,
                device_id_type=MESH,
            )

        @pl.loop(0, STEPS)
        def _(s):
            surface, eastward, southward = st[0], st[1], st[2]
            level = new_level(surface, eastward, southward, 0.0, 0.0)
            fluxes = new_fluxes(eastward, southward, level, 0.0, 0.0, depth, opened)
            tmp[0] = level
            tmp[1] = fluxes[0]
            tmp[2] = fluxes[1]

            @pl.when(s == 0)
            def _():
                first_out[0] = pack_strips(st)
                first_out[1] = pack_strips(tmp)
                peers = jnp.int32(tiles)
                for present, _device in links:
                    peers = peers + jnp.where(present, 1, 0)
                pl.semaphore_wait(barrier, peers)
                send_all(first_out, first_in.at[tile], first_sems.at[0], first_sems.at[1])

            @pl.when(s < STEPS - 1)
            def _():
                cols = iota((height, width), 1)
                rows = iota((height, width), 0)
                east_gap = fluxes[0] - jnp.where(cols == 0, 0.0, pltpu.roll(fluxes[0], 1, 1))
                south_gap = fluxes[1] - jnp.where(rows == 0, 0.0, pltpu.roll(fluxes[1], 1, 0))
                tmp[3] = level - COURANT * (east_gap + south_gap)
                tmp[4] = level - COURANT * (fluxes[0] + south_gap)
                tmp[5] = level - COURANT * (east_gap + fluxes[1])
                ring_out[s] = pack_ring(
                    [(tmp, (3,), -1), (tmp, (1,), -1), (tmp, (4,), PW)],
                    [(tmp, (3,), -1), (tmp, (2,), -1), (tmp, (5,), PH)],
                )
                send_all(ring_out.at[s], ring_in.at[s, tile], ring_send.at[s], ring_recv.at[s])

            @pl.when(s == 0)
            def _():
                fixed_out[...] = pack_ring(
                    [(depth_ref, (0, 0), -1), (open_ref, (0, 0), -1)],
                    [(depth_ref, (0, 1), -1), (open_ref, (0, 1), -1)],
                )
                send_all(fixed_out, fixed_in.at[tile], fixed_sems.at[0], fixed_sems.at[1])

            east_out[s] = fold_column(eastward, width - 1)
            south_out[s] = southward[height - 8 :]
            to_east = halo(s, 0, east_out.at[s], west_in.at[s], east)
            to_south = halo(s, 1, south_out.at[s], north_in.at[s], south)
            to_west = halo(s, 2, west_out.at[s], east_in.at[s], west)
            to_north = halo(s, 3, level_out.at[s], south_in.at[s], north)

            @pl.when(has_east)
            def _():
                to_east.start()

            @pl.when(has_south)
            def _():
                to_south.start()

            @pl.when(has_west)
            def _():
                to_east.wait_recv()

            @pl.when(has_north)
            def _():
                to_south.wait_recv()

            level = new_level(
                surface,
                eastward,
                southward,
                unfold_column(west_in[s], height),
                north_in[s][7:8, :],
            )
            level_out[s] = level[0:8]
            west_out[s] = fold_column(level, 0)

            @pl.when(has_west)
            def _():
                to_west.start()

            @pl.when(has_north)
            def _():
                to_north.start()

            @pl.when(has_east)
            def _():
                to_west.wait_recv()

            @pl.when(has_south)
            def _():
                to_north.wait_recv()

            fluxes = new_fluxes(
                eastward, southward, level, unfold_column(east_in[s], height), south_in[s][0:1, :], depth, opened
            )
            st[0] = level
            st[1] = fluxes[0]
            st[2] = fluxes[1]

            wait_all(ret_in.at[s], ret_recv.at[s])
            ret_now[...] = ret_in[s]
            lane = iota((PH, width), 1)
            for band in range(K):
                first = band * FINE_ROWS + TOP
                merged = [st[f, first : first + PH, :] for f in range(3)]
                for j in range(RR - 1):
                    p = band * (RR - 1) + j
                    column = LEFT + j * PW
                    block = ret_now[slots[p]]
                    mask = (
                        (lane >= column)
                        & (lane < column + PW)
                        & (jnp.full((PH, width), covers[p], jnp.int32) > 0)
                    )
                    for f in range(3):
                        shifted = pltpu.roll(block, (column - f * PW) % width, 1)
                        merged[f] = jnp.where(mask, shifted, merged[f])
                for f in range(3):
                    st[f, first : first + PH, :] = merged[f]

        out_ref[0] = st[...]

        for s in range(STEPS):

            @pl.when(has_east)
            def _():
                halo(s, 0, east_out.at[s], west_in.at[s], east).wait_send()

            @pl.when(has_south)
            def _():
                halo(s, 1, south_out.at[s], north_in.at[s], south).wait_send()

            @pl.when(has_west)
            def _():
                halo(s, 2, west_out.at[s], east_in.at[s], west).wait_send()

            @pl.when(has_north)
            def _():
                halo(s, 3, level_out.at[s], south_in.at[s], north).wait_send()

        wait_all(first_in, first_sems.at[0])
        wait_all(fixed_in, fixed_sems.at[0])
        for s in range(STEPS - 1):
            wait_all(ring_in.at[s], ring_send.at[s])

    @pl.when(jnp.logical_not(is_outer))
    def _():
        @pl.loop(0, tiles - 1)
        def _(i):
            t = lax.rem(tile + i + 1, tiles)
            pl.semaphore_signal(
                barrier, inc=1, device_id=(sec, t // n_nest, lax.rem(t, n_nest)), device_id_type=MESH
            )

        spots, lives = [], []
        for k in range(K):
            spot, live = jnp.int32(0), jnp.int32(0)
            for n in range(nests):
                hit = host_ref[n] == tile * K + k
                spot = jnp.where(hit, place_ref[n], spot)
                live = jnp.where(hit, 1, live)
            spots.append(spot)
            lives.append(live)
        homes = [spot // NPOS for spot in spots]
        bands = [lax.rem(spot, NPOS) // (RR - 1) for spot in spots]
        columns = [lax.rem(spot, RR - 1) for spot in spots]
        near = []
        for k in range(K):
            pair = []
            for side in (-1, 1):
                inside = (columns[k] + side >= 0) & (columns[k] + side < RR - 1)
                slot, cover = jnp.int32(0), jnp.int32(0)
                for n in range(nests):
                    hit = inside & (place_ref[n] == spots[k] + side)
                    slot = jnp.where(hit, host_ref[n], slot)
                    cover = jnp.where(hit, 1, cover)
                pair.append((slot // K, lax.rem(slot, K), cover))
            near.append(pair)
        for k in range(K):
            source = iota((width, width), 0)
            fine = iota((width, width), 1)
            wanted = LEFT + columns[k] * PW + fine // RR
            spread[k] = (source == wanted).astype(jnp.float32).astype(jnp.bfloat16)
        grow = (iota((FINE_ROWS, PH), 0) // RR == iota((FINE_ROWS, PH), 1)).astype(jnp.float32)
        gather_from = iota((3 * width, 2 * width), 0)
        gather_to = iota((3 * width, 2 * width), 1)
        field, lane_in = gather_from // width, lax.rem(gather_from, width)
        weight = jnp.where(
            field == 1, jnp.where(lax.rem(lane_in, RR) == RR - 1, 1.0, 0.0), 1.0 / RR
        )
        gather = jnp.where(gather_to == field * PW + lane_in // RR, weight, 0.0)
        for i, (f, c) in enumerate(EDGES):
            gather = gather + jnp.where(
                (gather_to >= width)
                & (lax.rem(gather_to, 8 * K) == i)
                & (field == f)
                & (lane_in // RR == c),
                weight,
                0.0,
            )
        fold_to = iota((width, width), 1)
        fold = (
            (lax.rem(iota((width, width), 0), 8 * K) == fold_to) & (fold_to < 8 * K)
        ).astype(jnp.float32)
        widen_to = iota((width, 3 * width), 1)
        widen = (
            iota((width, 3 * width), 0)
            == (widen_to // width) * PW + lax.rem(widen_to, width) // RR
        ).astype(jnp.float32)
        shrink_row = iota((2 * PH, FINE_ROWS), 0)
        shrink_from = iota((2 * PH, FINE_ROWS), 1)
        shrink = jnp.where(
            shrink_row < PH,
            jnp.where(shrink_from // RR == shrink_row, 1.0 / RR, 0.0),
            jnp.where(shrink_from == (shrink_row - PH) * RR + RR - 1, 1.0, 0.0),
        )

        grow, shrink, gather, fold, widen = [
            m.astype(jnp.bfloat16) for m in (grow, shrink, gather, fold, widen)
        ]

        def side_ghosts(block, k):
            lane, sub = iota((PH, width), 1), iota((PH, width), 0)
            tall_lane = iota((FINE_ROWS, width), 1)
            tall = dot_of(grow, block)
            wide = dot_by(block, spread[k])
            west_lane = bands[k] * (2 * (RR - 1)) + columns[k]
            west = jnp.sum(jnp.where(tall_lane == west_lane, tall, 0.0), axis=1, keepdims=True)
            east = jnp.sum(
                jnp.where(tall_lane == west_lane + (RR - 1), tall, 0.0), axis=1, keepdims=True
            )
            north = jnp.sum(jnp.where(sub == 2 * bands[k], wide, 0.0), axis=0, keepdims=True)
            south = jnp.sum(jnp.where(sub == 2 * bands[k] + 1, wide, 0.0), axis=0, keepdims=True)
            return west, north, east, south

        def keep(buffer, k, sides):
            west, north, east, south = sides
            lane = iota((FINE_ROWS, width), 1)
            buffer[k, 0:FINE_ROWS] = jnp.where(lane == 0, west, east)
            buffer[k, FINE_ROWS : FINE_ROWS + 8] = jnp.where(
                iota((8, width), 0) == 0, north, south
            )

        def kept(buffer, k):
            return (
                buffer[k, 0:FINE_ROWS][:, 0:1],
                buffer[k, FINE_ROWS : FINE_ROWS + 1],
                buffer[k, 0:FINE_ROWS][:, 1:2],
                buffer[k, FINE_ROWS + 1 : FINE_ROWS + 2],
            )

        def pick_lane(tall, index):
            lane = iota(tall.shape, 1)
            return jnp.sum(jnp.where(lane == index, tall, 0.0), axis=1, keepdims=True)

        def pick_row(wide, index):
            sub = iota(wide.shape, 0)
            return jnp.sum(jnp.where(sub == index, wide, 0.0), axis=0, keepdims=True)

        def ring_terms(k):
            ring = ring_now[homes[k]]
            tall, wide = dot_of(grow, ring), dot_by(ring, spread[k])
            base = bands[k] * (LEFT + (RR - 1) * PW) + 3 * columns[k]
            sides = [pick_lane(tall, base + i) for i in range(3)]
            lines = [pick_row(wide, 3 * bands[k] + i) for i in range(3)]
            flux_line = pick_row(ring, 3 * bands[k] + 1)
            first = LEFT + columns[k] * PW
            corners = [pick_lane(flux_line, first - 1), pick_lane(flux_line, first + PW)]
            return sides, lines, corners

        def next_sides(k, own, ring):
            (level_w, flux_w, level_e), (level_n, flux_n, level_s), (corner_w, corner_e) = ring
            surface, eastward, southward = [own[:, f * width : (f + 1) * width] for f in range(3)]
            depth_w, depth_n, open_w, open_n = kept(fixed_terms, k)

            taken = []
            for device, slot, cover in near[k]:
                line = jnp.broadcast_to(edge_now[device, 0:1], (FINE_ROWS, width))
                own_row = iota((FINE_ROWS, width), 1) // (8 * K) == iota((FINE_ROWS, width), 0) // RR
                edges = dot_by(jnp.where(own_row, line, 0.0), fold)
                chosen = edges
                for other in range(1, K):
                    chosen = jnp.where(
                        jnp.full(edges.shape, slot, jnp.int32) == other,
                        pltpu.roll(edges, width - 8 * other, 1),
                        chosen,
                    )
                taken.append((chosen, jnp.full((FINE_ROWS, 1), cover, jnp.int32) > 0))
            (left, has_left), (right, has_right) = taken
            s_l, e_l, e_p, q_l = [left[:, i : i + 1] for i in range(4)]
            s_f, e_f, q_f = [right[:, i : i + 1] for i in range(4, 7)]
            left_level = s_l - COURANT * ((e_l - e_p) + (q_l - below(q_l, corner_w)))
            right_level = s_f - COURANT * (e_f + (q_f - below(q_f, corner_e)))
            level_w = jnp.where(has_left, left_level, level_w)
            flux_w = jnp.where(has_left, e_l, flux_w)
            level_e = jnp.where(has_right, right_level, level_e)

            cols, rows = iota((FINE_ROWS, width), 1), iota((FINE_ROWS, width), 0)
            behind = jnp.where(cols < RR, flux_w, pltpu.roll(eastward, RR, 1))
            above = jnp.where(rows < RR, flux_n, pltpu.roll(southward, RR, 0))
            level = surface - COURANT * ((eastward - behind) + (southward - above))
            west_cell = level[:, 0:1]
            north_cell = level[0:1, :]
            west = open_w * (
                flux_w - COURANT * (depth_w + 0.5 * (level_w + west_cell)) * (west_cell - level_w)
            )
            north = open_n * (
                flux_n - COURANT * (depth_n + 0.5 * (level_n + north_cell)) * (north_cell - level_n)
            )
            east = level_e + COURANT * eastward[:, width - 1 : width]
            south = level_s + COURANT * southward[FINE_ROWS - 1 : FINE_ROWS, :]
            return west, north, east, south

        def below(column, top):
            wide = jnp.broadcast_to(column, (FINE_ROWS, width))
            rows = iota((FINE_ROWS, width), 0)
            return jnp.where(rows < RR, top, pltpu.roll(wide, RR, 0))[:, 0:1]

        for load in loads:
            load.wait()
        st[...] = state_ref[0]
        pl.semaphore_wait(barrier, 2 * tiles - 1)
        wait_all(first_in, first_sems.at[1])
        for k in range(K):
            keep(ghosts.at[0], k, side_ghosts(first_in[homes[k], 0], k))
            keep(ghosts.at[1], k, side_ghosts(first_in[homes[k], 1], k))

        @pl.loop(0, STEPS)
        def _(s):
            edge = jnp.zeros((PH, width), jnp.float32)
            lane = iota((PH, width), 1)
            for k in range(K):
                slot = pl.ds(k * FINE_ROWS, FINE_ROWS)
                old, new = kept(ghosts.at[0], k), kept(ghosts.at[1], k)
                surface, eastward, southward = st[0, slot], st[1, slot], st[2, slot]
                depth = [depth_ref[0, i, slot] for i in range(2)]
                opened = [open_ref[0, i, slot].astype(jnp.float32) for i in range(2)]
                for m in range(1, RR + 1):
                    west_g, north_g, east_g, south_g = [
                        a + (m / RR) * (b - a) for a, b in zip(old, new)
                    ]
                    surface = new_level(surface, eastward, southward, west_g, north_g)
                    eastward, southward = new_fluxes(
                        eastward, southward, surface, east_g, south_g, depth, opened
                    )
                st[0, slot] = surface
                st[1, slot] = eastward
                st[2, slot] = southward
                packed = dot_by(jnp.concatenate([surface, eastward, southward], axis=1), gather)
                both = dot_of(shrink, packed)
                block = jnp.where(
                    lane < 2 * PW, both[0:PH, 0:width], both[PH : 2 * PH, 0:width]
                )
                ret_out[s, k] = block
                ret_now[k] = block
                spot = lax.rem(lane, 8 * K)
                mean = spot < 0
                for i, (f, c) in enumerate(EDGES):
                    if f < 2:
                        mean = mean | (spot == i)
                side = jnp.where(mean, both[0:PH, width:], both[PH : 2 * PH, width:])
                side = jnp.where(lane // (8 * K) == iota((PH, width), 0), side, 0.0)
                edge = edge + pltpu.roll(side, 8 * k, 1)

            @pl.when(s < STEPS - 1)
            def _():
                edge_out[s, 0:1] = jnp.sum(edge, axis=0, keepdims=True)
                send_to(
                    1,
                    tiles - 1,
                    edge_out.at[s, pl.ds(0, 1)],
                    edge_in.at[s, tile, pl.ds(0, 1)],
                    edge_send.at[s],
                    edge_recv.at[s],
                )

            send_all(ret_out.at[s], ret_in.at[s, pl.ds(tile * K, K)], ret_send.at[s], ret_recv.at[s])

            @pl.when(s == 0)
            def _():
                wait_all(fixed_in, fixed_sems.at[1])
                for k in range(K):
                    fixed = fixed_in[homes[k]]
                    tall, wide = dot_of(grow, fixed), dot_by(fixed, spread[k])
                    base = bands[k] * (LEFT + (RR - 1) * PW) + 3 * columns[k]
                    keep(
                        fixed_terms,
                        k,
                        (
                            pick_lane(tall, base),
                            pick_row(wide, 3 * bands[k]),
                            pick_lane(tall, base + 1),
                            pick_row(wide, 3 * bands[k] + 1),
                        ),
                    )

            @pl.when(s < STEPS - 1)
            def _():
                owns = []
                for k in range(K):
                    ghosts[0, k] = ghosts[1, k]
                    owns.append(dot_by(dot_of(grow, ret_now[k]), widen))
                wait_all(ring_in.at[s], ring_recv.at[s])
                ring_now[...] = ring_in[s]
                rings = [ring_terms(k) for k in range(K)]
                wait_all(edge_in.at[s, pl.ds(0, tiles - 1), pl.ds(0, 1)], edge_recv.at[s])
                edge_now[:, 0:1] = edge_in[s, :, 0:1]
                edge_now[tile, 0:1] = edge_out[s, 0:1]
                for k in range(K):
                    keep(ghosts.at[1], k, next_sides(k, owns[k], rings[k]))

        for k in range(K):
            slot = pl.ds(k * FINE_ROWS, FINE_ROWS)
            live = jnp.full((FINE_ROWS, width), lives[k], jnp.int32) > 0
            for f in range(3):
                out_ref[0, f, slot] = jnp.where(live, st[f, slot], state_ref[0, f, slot])

        for s in range(STEPS):
            wait_all(ret_in.at[s], ret_send.at[s])
        for s in range(STEPS - 1):
            wait_all(edge_in.at[s, pl.ds(0, tiles - 1), pl.ds(0, 1)], edge_send.at[s])


def on_device(n_row, n_nest, ocean_state, face_depth, face_open, nest_place, nest_host):
    tiles = n_row * n_nest
    height, width = ocean_state.shape[2:]
    f32 = jnp.float32
    vmem = pl.BlockSpec(memory_space=pltpu.VMEM)
    hbm = pl.BlockSpec(memory_space=pl.ANY)
    smem = pl.BlockSpec(memory_space=pltpu.SMEM)
    dma = pltpu.SemaphoreType.DMA
    return pl.pallas_call(
        functools.partial(kernel, n_row, n_nest),
        out_shape=jax.ShapeDtypeStruct(ocean_state.shape, f32),
        in_specs=[smem, smem, hbm, hbm, hbm],
        out_specs=vmem,
        scratch_shapes=[
            pltpu.VMEM(ocean_state.shape, f32),
            pltpu.VMEM(face_depth.shape, f32),
            pltpu.VMEM(face_open.shape, jnp.int32),
            dma((3,)),
            pltpu.VMEM((3, height, width), f32),
            pltpu.VMEM((6, height, width), f32),
            pltpu.VMEM((2, PH, width), f32),
            pltpu.VMEM((tiles, 2, PH, width), f32),
            pltpu.VMEM((PH, width), f32),
            pltpu.VMEM((tiles, PH, width), f32),
            pltpu.VMEM((STEPS - 1, PH, width), f32),
            pltpu.VMEM((STEPS - 1, tiles, PH, width), f32),
            pltpu.VMEM((STEPS - 1, PH, width), f32),
            pltpu.VMEM((STEPS - 1, tiles, PH, width), f32),
            pltpu.VMEM((STEPS, K, PH, width), f32),
            pltpu.VMEM((STEPS, tiles * K, PH, width), f32),
            pltpu.VMEM((STEPS, 8, width), f32),
            pltpu.VMEM((STEPS, 8, width), f32),
            pltpu.VMEM((STEPS, 8, width), f32),
            pltpu.VMEM((STEPS, 8, width), f32),
            pltpu.VMEM((STEPS, 8, width), f32),
            pltpu.VMEM((STEPS, 8, width), f32),
            pltpu.VMEM((STEPS, 8, width), f32),
            pltpu.VMEM((STEPS, 8, width), f32),
            pltpu.VMEM((K, width, width), jnp.bfloat16),
            pltpu.VMEM((2, K, FINE_ROWS + 8, width), f32),
            pltpu.VMEM((tiles, PH, width), f32),
            pltpu.VMEM((tiles, PH, width), f32),
            pltpu.VMEM((tiles * K, PH, width), f32),
            pltpu.VMEM((K, FINE_ROWS + 8, width), f32),
            dma((2,)),
            dma((2,)),
            dma((STEPS - 1,)),
            dma((STEPS - 1,)),
            dma((STEPS - 1,)),
            dma((STEPS - 1,)),
            dma((STEPS,)),
            dma((STEPS,)),
            dma((STEPS, 4)),
            dma((STEPS, 4)),
        ],
        compiler_params=pltpu.CompilerParams(collective_id=0, has_side_effects=True),
    )(nest_place, nest_host, ocean_state, face_depth, face_open)


def solution(mesh):
    field = P("sec", None, "row", "nest")
    return jax.shard_map(
        functools.partial(on_device, mesh.shape["row"], mesh.shape["nest"]),
        mesh=mesh,
        in_specs=(field, field, field, P(), P()),
        out_specs=field,
        check_vma=False,
    )
```

```python
import functools

import jax
import jax.numpy as jnp
from jax import lax
from jax.experimental import pallas as pl
from jax.experimental.pallas import tpu as pltpu
from jax.sharding import PartitionSpec as P

PH = 8
PW = 32
RR = 4
K = 2
STEPS = 4
NPOS = K * (RR - 1)
COURANT = 0.3
MESH = pl.DeviceIdType.MESH
FINE_ROWS = RR * PH
TOP = (RR - 1) * PH // 2
LEFT = PW // 2
EDGES = ((0, PW - 1), (1, PW - 1), (1, PW - 2), (2, PW - 1), (0, 0), (1, 0), (2, 0))


def iota(shape, dim):
    return lax.broadcasted_iota(jnp.int32, shape, dim)


def new_level(surface, eastward, southward, west_ghost, north_ghost):
    rows, cols = iota(surface.shape, 0), iota(surface.shape, 1)
    east_behind = jnp.where(cols == 0, west_ghost, pltpu.roll(eastward, 1, 1))
    south_behind = jnp.where(rows == 0, north_ghost, pltpu.roll(southward, 1, 0))
    return surface - COURANT * ((eastward - east_behind) + (southward - south_behind))


def new_fluxes(eastward, southward, level, east_ghost, south_ghost, depth, opened):
    height, width = level.shape
    rows, cols = iota(level.shape, 0), iota(level.shape, 1)
    level_east = jnp.where(cols == width - 1, east_ghost, pltpu.roll(level, width - 1, 1))
    level_south = jnp.where(rows == height - 1, south_ghost, pltpu.roll(level, height - 1, 0))
    east = opened[0] * (
        eastward - COURANT * (depth[0] + 0.5 * (level + level_east)) * (level_east - level)
    )
    south = opened[1] * (
        southward - COURANT * (depth[1] + 0.5 * (level + level_south)) * (level_south - level)
    )
    return east, south


def parts(x):
    high = x.astype(jnp.bfloat16).astype(jnp.float32)
    rest = x - high
    middle = rest.astype(jnp.bfloat16).astype(jnp.float32)
    return high, middle, rest - middle


def dot_by(x, chosen):
    rows = x.shape[0]
    stacked = jnp.concatenate(parts(x), axis=0).astype(jnp.bfloat16)
    y = jnp.dot(stacked, chosen, preferred_element_type=jnp.float32)
    return y[:rows] + (y[rows : 2 * rows] + y[2 * rows :])


def dot_of(chosen, x):
    cols = x.shape[1]
    stacked = jnp.concatenate(parts(x), axis=1).astype(jnp.bfloat16)
    y = jnp.dot(chosen, stacked, preferred_element_type=jnp.float32)
    return y[:, :cols] + (y[:, cols : 2 * cols] + y[:, 2 * cols :])


def pack_strips(tmp):
    width = tmp.shape[2]
    lane, sub = iota((PH, width), 1), iota((PH, width), 0)
    block = jnp.zeros((PH, width), jnp.float32)
    span = (RR - 1) * PW
    inner = (lane >= LEFT) & (lane < LEFT + span)
    for band in range(K):
        first = band * FINE_ROWS + TOP
        east8 = tmp[1, first : first + PH, :]
        level8 = tmp[0, first : first + PH, :]
        for j in range(RR - 1):
            column = LEFT + j * PW
            west_lane = band * 2 * (RR - 1) + j
            east_lane = west_lane + RR - 1
            block = jnp.where(
                lane == west_lane, pltpu.roll(east8, (west_lane - column + 1) % width, 1), block
            )
            block = jnp.where(
                lane == east_lane, pltpu.roll(level8, (east_lane - column - PW) % width, 1), block
            )
        block = jnp.where(inner & (sub == 2 * band), tmp[2, first - 1 : first, :], block)
        block = jnp.where(inner & (sub == 2 * band + 1), tmp[0, first + PH : first + PH + 1, :], block)
    return block


def pack_ring(sides, lines):
    ref, width = sides[0][0], sides[0][0].shape[-1]
    lane, sub = iota((PH, width), 1), iota((PH, width), 0)
    span = (RR - 1) * PW
    block = jnp.zeros((PH, width), jnp.float32)
    inner = (lane >= LEFT) & (lane < LEFT + span)
    for band in range(K):
        first = band * FINE_ROWS + TOP
        base = band * (LEFT + span)
        for i, (ref, index, shift) in enumerate(sides):
            values = ref[index + (slice(first, first + PH), slice(None))].astype(jnp.float32)
            for j in range(RR - 1):
                target = base + 3 * j + i
                source = LEFT + j * PW + shift
                block = jnp.where(
                    lane == target, pltpu.roll(values, (target - source) % width, 1), block
                )
        for i, (ref, index, shift) in enumerate(lines):
            at = first + shift
            line = ref[index + (slice(at, at + 1), slice(None))].astype(jnp.float32)
            block = jnp.where(inner & (sub == 3 * band + i), line, block)
    return block


def fold_column(field, column):
    height, width = field.shape
    lane = iota((8, width), 1)
    block = jnp.zeros((8, width), jnp.float32)
    for v in range(height // 8):
        piece = pltpu.roll(field[8 * v : 8 * v + 8], (v - column) % width, 1)
        block = jnp.where(lane == v, piece, block)
    return block


def unfold_column(block, height):
    return jnp.concatenate([block[:, v : v + 1] for v in range(height // 8)], axis=0)


def kernel(
    n_row,
    n_nest,
    place_ref,
    host_ref,
    state_hbm,
    depth_hbm,
    open_hbm,
    out_ref,
    state_ref,
    depth_ref,
    open_ref,
    load_sems,
    st,
    tmp,
    first_out,
    first_in,
    fixed_out,
    fixed_in,
    ring_out,
    ring_in,
    edge_out,
    edge_in,
    ret_out,
    ret_in,
    east_out,
    south_out,
    level_out,
    west_out,
    west_in,
    north_in,
    east_in,
    south_in,
    spread,
    ghosts,
    ring_now,
    edge_now,
    ret_now,
    fixed_terms,
    first_sems,
    fixed_sems,
    ring_send,
    ring_recv,
    edge_send,
    edge_recv,
    ret_send,
    ret_recv,
    halo_send,
    halo_recv,
):
    tiles = n_row * n_nest
    nests = place_ref.shape[0]
    sec, row, col = lax.axis_index("sec"), lax.axis_index("row"), lax.axis_index("nest")
    tile = row * n_nest + col
    is_outer = sec == 0
    has_west, has_east = col > 0, col < n_nest - 1
    has_north, has_south = row > 0, row < n_row - 1
    west, east = (sec, row, col - 1), (sec, row, col + 1)
    north, south = (sec, row - 1, col), (sec, row + 1, col)
    links = ((has_west, west), (has_east, east), (has_north, north), (has_south, south))
    height, width = state_ref.shape[2], state_ref.shape[3]

    barrier = pltpu.get_barrier_semaphore()

    @pl.loop(0, tiles)
    def _(i):
        t = lax.rem(tile + i, tiles)
        pl.semaphore_signal(
            barrier, inc=1, device_id=(1 - sec, t // n_nest, lax.rem(t, n_nest)), device_id_type=MESH
        )

    loads = [
        pltpu.make_async_copy(source, target, load_sems.at[i])
        for i, (source, target) in enumerate(
            ((state_hbm, state_ref), (depth_hbm, depth_ref), (open_hbm, open_ref))
        )
    ]
    for load in loads:
        load.start()

    def send_to(section, count, src, dst, send_sem, recv_sem):
        @pl.loop(0, tiles)
        def _(i):
            t = lax.rem(2 * tiles - 1 - tile - i, tiles)

            def go():
                pltpu.make_async_remote_copy(
                    src_ref=src,
                    dst_ref=dst,
                    send_sem=send_sem,
                    recv_sem=recv_sem,
                    device_id=(section, t // n_nest, lax.rem(t, n_nest)),
                    device_id_type=MESH,
                ).start()

            if count == tiles:
                go()
            else:
                pl.when(t != tile)(go)

    def send_all(src, dst, send_sem, recv_sem):
        send_to(1 - sec, tiles, src, dst, send_sem, recv_sem)

    def wait_all(whole, sem):
        pltpu.make_async_copy(whole, whole, sem).wait()

    @pl.when(is_outer)
    def _():
        for present, device in links:

            @pl.when(present)
            def _():
                pl.semaphore_signal(barrier, inc=1, device_id=device, device_id_type=MESH)

        for load in loads:
            load.wait()
        st[...] = state_ref[0]
        depth = [depth_ref[0, i] for i in range(2)]
        opened = [open_ref[0, i].astype(jnp.float32) for i in range(2)]
        slots, covers = [], []
        for p in range(NPOS):
            slot, cover = jnp.int32(0), jnp.int32(0)
            for n in range(nests):
                hit = place_ref[n] == tile * NPOS + p
                slot = jnp.where(hit, host_ref[n], slot)
                cover = jnp.where(hit, 1, cover)
            slots.append(slot)
            covers.append(cover)
        zero_block = jnp.zeros((height, width), jnp.float32)
        for present, buffer in (
            (has_west, west_in),
            (has_east, east_in),
            (has_north, north_in),
            (has_south, south_in),
        ):

            @pl.when(jnp.logical_not(present))
            def _():
                for s in range(STEPS):
                    buffer[s] = jnp.zeros(buffer.shape[1:], jnp.float32)

        def halo(s, kind, src, dst, device):
            return pltpu.make_async_remote_copy(
                src_ref=src,
                dst_ref=dst,
                send_sem=halo_send.at[s, kind],
                recv_sem=halo_recv.at[s, kind],
                device_id=device,
                device_id_type=MESH,
            )

        @pl.loop(0, STEPS)
        def _(s):
            for band in range(K):
                lo = band * FINE_ROWS + (TOP - 3) // 8 * 8
                hi = band * FINE_ROWS + (TOP + PH + 3 + 7) // 8 * 8
                old = [st[f, lo:hi] for f in range(3)]
                level = new_level(old[0], old[1], old[2], 0.0, 0.0)
                flux_e, flux_s = new_fluxes(
                    old[1],
                    old[2],
                    level,
                    0.0,
                    0.0,
                    [d[lo:hi] for d in depth],
                    [o[lo:hi] for o in opened],
                )
                east_gap = flux_e - pltpu.roll(flux_e, 1, 1)
                south_gap = flux_s - pltpu.roll(flux_s, 1, 0)
                tmp[0, lo:hi] = level
                tmp[1, lo:hi] = flux_e
                tmp[2, lo:hi] = flux_s
                tmp[3, lo:hi] = level - COURANT * (east_gap + south_gap)
                tmp[4, lo:hi] = level - COURANT * (flux_e + south_gap)
                tmp[5, lo:hi] = level - COURANT * (east_gap + flux_s)

            @pl.when(s == 0)
            def _():
                first_out[0] = pack_strips(st)
                first_out[1] = pack_strips(tmp)
                peers = jnp.int32(tiles)
                for present, _device in links:
                    peers = peers + jnp.where(present, 1, 0)
                pl.semaphore_wait(barrier, peers)
                send_all(first_out, first_in.at[tile], first_sems.at[0], first_sems.at[1])

            @pl.when(s < STEPS - 1)
            def _():
                ring_out[s] = pack_ring(
                    [(tmp, (3,), -1), (tmp, (1,), -1), (tmp, (4,), PW)],
                    [(tmp, (3,), -1), (tmp, (2,), -1), (tmp, (5,), PH)],
                )
                send_all(ring_out.at[s], ring_in.at[s, tile], ring_send.at[s], ring_recv.at[s])

            @pl.when(s == 0)
            def _():
                fixed_out[...] = pack_ring(
                    [(depth_ref, (0, 0), -1), (open_ref, (0, 0), -1)],
                    [(depth_ref, (0, 1), -1), (open_ref, (0, 1), -1)],
                )
                send_all(fixed_out, fixed_in.at[tile], fixed_sems.at[0], fixed_sems.at[1])

            surface, eastward, southward = st[0], st[1], st[2]
            east_out[s] = fold_column(eastward, width - 1)
            south_out[s] = southward[height - 8 :]
            to_east = halo(s, 0, east_out.at[s], west_in.at[s], east)
            to_south = halo(s, 1, south_out.at[s], north_in.at[s], south)
            to_west = halo(s, 2, west_out.at[s], east_in.at[s], west)
            to_north = halo(s, 3, level_out.at[s], south_in.at[s], north)

            @pl.when(has_east)
            def _():
                to_east.start()

            @pl.when(has_south)
            def _():
                to_south.start()

            @pl.when(has_west)
            def _():
                to_east.wait_recv()

            @pl.when(has_north)
            def _():
                to_south.wait_recv()

            level = new_level(
                surface,
                eastward,
                southward,
                unfold_column(west_in[s], height),
                north_in[s][7:8, :],
            )
            level_out[s] = level[0:8]
            west_out[s] = fold_column(level, 0)

            @pl.when(has_west)
            def _():
                to_west.start()

            @pl.when(has_north)
            def _():
                to_north.start()

            @pl.when(has_east)
            def _():
                to_west.wait_recv()

            @pl.when(has_south)
            def _():
                to_north.wait_recv()

            fluxes = new_fluxes(
                eastward, southward, level, unfold_column(east_in[s], height), south_in[s][0:1, :], depth, opened
            )
            st[0] = level
            st[1] = fluxes[0]
            st[2] = fluxes[1]

            wait_all(ret_in.at[s], ret_recv.at[s])
            ret_now[...] = ret_in[s]
            lane = iota((PH, width), 1)
            for band in range(K):
                first = band * FINE_ROWS + TOP
                merged = [st[f, first : first + PH, :] for f in range(3)]
                for j in range(RR - 1):
                    p = band * (RR - 1) + j
                    column = LEFT + j * PW
                    block = ret_now[slots[p]]
                    mask = (
                        (lane >= column)
                        & (lane < column + PW)
                        & (jnp.full((PH, width), covers[p], jnp.int32) > 0)
                    )
                    for f in range(3):
                        shifted = pltpu.roll(block, (column - f * PW) % width, 1)
                        merged[f] = jnp.where(mask, shifted, merged[f])
                for f in range(3):
                    st[f, first : first + PH, :] = merged[f]

        out_ref[0] = st[...]

        for s in range(STEPS):

            @pl.when(has_east)
            def _():
                halo(s, 0, east_out.at[s], west_in.at[s], east).wait_send()

            @pl.when(has_south)
            def _():
                halo(s, 1, south_out.at[s], north_in.at[s], south).wait_send()

            @pl.when(has_west)
            def _():
                halo(s, 2, west_out.at[s], east_in.at[s], west).wait_send()

            @pl.when(has_north)
            def _():
                halo(s, 3, level_out.at[s], south_in.at[s], north).wait_send()

        wait_all(first_in, first_sems.at[0])
        wait_all(fixed_in, fixed_sems.at[0])
        for s in range(STEPS - 1):
            wait_all(ring_in.at[s], ring_send.at[s])

    @pl.when(jnp.logical_not(is_outer))
    def _():
        @pl.loop(0, tiles - 1)
        def _(i):
            t = lax.rem(tile + i + 1, tiles)
            pl.semaphore_signal(
                barrier, inc=1, device_id=(sec, t // n_nest, lax.rem(t, n_nest)), device_id_type=MESH
            )

        spots, lives = [], []
        for k in range(K):
            spot, live = jnp.int32(0), jnp.int32(0)
            for n in range(nests):
                hit = host_ref[n] == tile * K + k
                spot = jnp.where(hit, place_ref[n], spot)
                live = jnp.where(hit, 1, live)
            spots.append(spot)
            lives.append(live)
        homes = [spot // NPOS for spot in spots]
        bands = [lax.rem(spot, NPOS) // (RR - 1) for spot in spots]
        columns = [lax.rem(spot, RR - 1) for spot in spots]
        near = []
        for k in range(K):
            pair = []
            for side in (-1, 1):
                inside = (columns[k] + side >= 0) & (columns[k] + side < RR - 1)
                slot, cover = jnp.int32(0), jnp.int32(0)
                for n in range(nests):
                    hit = inside & (place_ref[n] == spots[k] + side)
                    slot = jnp.where(hit, host_ref[n], slot)
                    cover = jnp.where(hit, 1, cover)
                pair.append((slot // K, lax.rem(slot, K), cover))
            near.append(pair)
        for k in range(K):
            source = iota((width, width), 0)
            fine = iota((width, width), 1)
            wanted = LEFT + columns[k] * PW + fine // RR
            spread[k] = (source == wanted).astype(jnp.float32).astype(jnp.bfloat16)
        grow = (iota((FINE_ROWS, PH), 0) // RR == iota((FINE_ROWS, PH), 1)).astype(jnp.float32)
        gather_from = iota((3 * width, 2 * width), 0)
        gather_to = iota((3 * width, 2 * width), 1)
        field, lane_in = gather_from // width, lax.rem(gather_from, width)
        weight = jnp.where(
            field == 1, jnp.where(lax.rem(lane_in, RR) == RR - 1, 1.0, 0.0), 1.0 / RR
        )
        gather = jnp.where(gather_to == field * PW + lane_in // RR, weight, 0.0)
        for i, (f, c) in enumerate(EDGES):
            gather = gather + jnp.where(
                (gather_to >= width)
                & (lax.rem(gather_to, 8 * K) == i)
                & (field == f)
                & (lane_in // RR == c),
                weight,
                0.0,
            )
        fold_to = iota((width, width), 1)
        fold = (
            (lax.rem(iota((width, width), 0), 8 * K) == fold_to) & (fold_to < 8 * K)
        ).astype(jnp.float32)
        widen_to = iota((width, 3 * width), 1)
        widen = (
            iota((width, 3 * width), 0)
            == (widen_to // width) * PW + lax.rem(widen_to, width) // RR
        ).astype(jnp.float32)
        shrink_row = iota((2 * PH, FINE_ROWS), 0)
        shrink_from = iota((2 * PH, FINE_ROWS), 1)
        shrink = jnp.where(
            shrink_row < PH,
            jnp.where(shrink_from // RR == shrink_row, 1.0 / RR, 0.0),
            jnp.where(shrink_from == (shrink_row - PH) * RR + RR - 1, 1.0, 0.0),
        )

        grow, shrink, gather, fold, widen = [
            m.astype(jnp.bfloat16) for m in (grow, shrink, gather, fold, widen)
        ]

        def side_ghosts(block, k):
            lane, sub = iota((PH, width), 1), iota((PH, width), 0)
            tall_lane = iota((FINE_ROWS, width), 1)
            tall = dot_of(grow, block)
            wide = dot_by(block, spread[k])
            west_lane = bands[k] * (2 * (RR - 1)) + columns[k]
            west = jnp.sum(jnp.where(tall_lane == west_lane, tall, 0.0), axis=1, keepdims=True)
            east = jnp.sum(
                jnp.where(tall_lane == west_lane + (RR - 1), tall, 0.0), axis=1, keepdims=True
            )
            north = jnp.sum(jnp.where(sub == 2 * bands[k], wide, 0.0), axis=0, keepdims=True)
            south = jnp.sum(jnp.where(sub == 2 * bands[k] + 1, wide, 0.0), axis=0, keepdims=True)
            return west, north, east, south

        def keep(buffer, k, sides):
            west, north, east, south = sides
            lane = iota((FINE_ROWS, width), 1)
            buffer[k, 0:FINE_ROWS] = jnp.where(lane == 0, west, east)
            buffer[k, FINE_ROWS : FINE_ROWS + 8] = jnp.where(
                iota((8, width), 0) == 0, north, south
            )

        def kept(buffer, k):
            return (
                buffer[k, 0:FINE_ROWS][:, 0:1],
                buffer[k, FINE_ROWS : FINE_ROWS + 1],
                buffer[k, 0:FINE_ROWS][:, 1:2],
                buffer[k, FINE_ROWS + 1 : FINE_ROWS + 2],
            )

        def pick_lane(tall, index):
            lane = iota(tall.shape, 1)
            return jnp.sum(jnp.where(lane == index, tall, 0.0), axis=1, keepdims=True)

        def pick_row(wide, index):
            sub = iota(wide.shape, 0)
            return jnp.sum(jnp.where(sub == index, wide, 0.0), axis=0, keepdims=True)

        def ring_terms(k):
            ring = ring_now[homes[k]]
            tall, wide = dot_of(grow, ring), dot_by(ring, spread[k])
            base = bands[k] * (LEFT + (RR - 1) * PW) + 3 * columns[k]
            sides = [pick_lane(tall, base + i) for i in range(3)]
            lines = [pick_row(wide, 3 * bands[k] + i) for i in range(3)]
            flux_line = pick_row(ring, 3 * bands[k] + 1)
            first = LEFT + columns[k] * PW
            corners = [pick_lane(flux_line, first - 1), pick_lane(flux_line, first + PW)]
            return sides, lines, corners

        def next_sides(k, own, ring):
            (level_w, flux_w, level_e), (level_n, flux_n, level_s), (corner_w, corner_e) = ring
            surface, eastward, southward = [own[:, f * width : (f + 1) * width] for f in range(3)]
            depth_w, depth_n, open_w, open_n = kept(fixed_terms, k)

            taken = []
            for device, slot, cover in near[k]:
                line = jnp.broadcast_to(edge_now[device, 0:1], (FINE_ROWS, width))
                own_row = iota((FINE_ROWS, width), 1) // (8 * K) == iota((FINE_ROWS, width), 0) // RR
                edges = dot_by(jnp.where(own_row, line, 0.0), fold)
                chosen = edges
                for other in range(1, K):
                    chosen = jnp.where(
                        jnp.full(edges.shape, slot, jnp.int32) == other,
                        pltpu.roll(edges, width - 8 * other, 1),
                        chosen,
                    )
                taken.append((chosen, jnp.full((FINE_ROWS, 1), cover, jnp.int32) > 0))
            (left, has_left), (right, has_right) = taken
            s_l, e_l, e_p, q_l = [left[:, i : i + 1] for i in range(4)]
            s_f, e_f, q_f = [right[:, i : i + 1] for i in range(4, 7)]
            left_level = s_l - COURANT * ((e_l - e_p) + (q_l - below(q_l, corner_w)))
            right_level = s_f - COURANT * (e_f + (q_f - below(q_f, corner_e)))
            level_w = jnp.where(has_left, left_level, level_w)
            flux_w = jnp.where(has_left, e_l, flux_w)
            level_e = jnp.where(has_right, right_level, level_e)

            cols, rows = iota((FINE_ROWS, width), 1), iota((FINE_ROWS, width), 0)
            behind = jnp.where(cols < RR, flux_w, pltpu.roll(eastward, RR, 1))
            above = jnp.where(rows < RR, flux_n, pltpu.roll(southward, RR, 0))
            level = surface - COURANT * ((eastward - behind) + (southward - above))
            west_cell = level[:, 0:1]
            north_cell = level[0:1, :]
            west = open_w * (
                flux_w - COURANT * (depth_w + 0.5 * (level_w + west_cell)) * (west_cell - level_w)
            )
            north = open_n * (
                flux_n - COURANT * (depth_n + 0.5 * (level_n + north_cell)) * (north_cell - level_n)
            )
            east = level_e + COURANT * eastward[:, width - 1 : width]
            south = level_s + COURANT * southward[FINE_ROWS - 1 : FINE_ROWS, :]
            return west, north, east, south

        def below(column, top):
            wide = jnp.broadcast_to(column, (FINE_ROWS, width))
            rows = iota((FINE_ROWS, width), 0)
            return jnp.where(rows < RR, top, pltpu.roll(wide, RR, 0))[:, 0:1]

        for load in loads:
            load.wait()
        st[...] = state_ref[0]
        pl.semaphore_wait(barrier, 2 * tiles - 1)
        wait_all(first_in, first_sems.at[1])
        for k in range(K):
            keep(ghosts.at[0], k, side_ghosts(first_in[homes[k], 0], k))
            keep(ghosts.at[1], k, side_ghosts(first_in[homes[k], 1], k))

        @pl.loop(0, STEPS)
        def _(s):
            edge = jnp.zeros((PH, width), jnp.float32)
            lane = iota((PH, width), 1)
            slots = [pl.ds(k * FINE_ROWS, FINE_ROWS) for k in range(K)]
            olds = [kept(ghosts.at[0], k) for k in range(K)]
            news = [kept(ghosts.at[1], k) for k in range(K)]
            fields = [[st[f, slot] for f in range(3)] for slot in slots]
            depths = [[depth_ref[0, i, slot] for i in range(2)] for slot in slots]
            opens = [[open_ref[0, i, slot].astype(jnp.float32) for i in range(2)] for slot in slots]
            for m in range(1, RR + 1):
                for k in range(K):
                    west_g, north_g, east_g, south_g = [
                        a + (m / RR) * (b - a) for a, b in zip(olds[k], news[k])
                    ]
                    surface, eastward, southward = fields[k]
                    surface = new_level(surface, eastward, southward, west_g, north_g)
                    eastward, southward = new_fluxes(
                        eastward, southward, surface, east_g, south_g, depths[k], opens[k]
                    )
                    fields[k] = [surface, eastward, southward]
            sums = [dot_by(jnp.concatenate(fields[k], axis=1), gather) for k in range(K)]
            sums = [dot_of(shrink, packed) for packed in sums]
            for k in range(K):
                for f in range(3):
                    st[f, slots[k]] = fields[k][f]
                both = sums[k]
                block = jnp.where(
                    lane < 2 * PW, both[0:PH, 0:width], both[PH : 2 * PH, 0:width]
                )
                ret_out[s, k] = block
                ret_now[k] = block
                spot = lax.rem(lane, 8 * K)
                mean = spot < 0
                for i, (f, c) in enumerate(EDGES):
                    if f < 2:
                        mean = mean | (spot == i)
                side = jnp.where(mean, both[0:PH, width:], both[PH : 2 * PH, width:])
                side = jnp.where(lane // (8 * K) == iota((PH, width), 0), side, 0.0)
                edge = edge + pltpu.roll(side, 8 * k, 1)

            @pl.when(s < STEPS - 1)
            def _():
                edge_out[s, 0:1] = jnp.sum(edge, axis=0, keepdims=True)
                send_to(
                    1,
                    tiles - 1,
                    edge_out.at[s, pl.ds(0, 1)],
                    edge_in.at[s, tile, pl.ds(0, 1)],
                    edge_send.at[s],
                    edge_recv.at[s],
                )

            send_all(ret_out.at[s], ret_in.at[s, pl.ds(tile * K, K)], ret_send.at[s], ret_recv.at[s])

            @pl.when(s == 0)
            def _():
                wait_all(fixed_in, fixed_sems.at[1])
                for k in range(K):
                    fixed = fixed_in[homes[k]]
                    tall, wide = dot_of(grow, fixed), dot_by(fixed, spread[k])
                    base = bands[k] * (LEFT + (RR - 1) * PW) + 3 * columns[k]
                    keep(
                        fixed_terms,
                        k,
                        (
                            pick_lane(tall, base),
                            pick_row(wide, 3 * bands[k]),
                            pick_lane(tall, base + 1),
                            pick_row(wide, 3 * bands[k] + 1),
                        ),
                    )

            @pl.when(s < STEPS - 1)
            def _():
                owns = []
                for k in range(K):
                    ghosts[0, k] = ghosts[1, k]
                    owns.append(dot_by(dot_of(grow, ret_now[k]), widen))
                wait_all(ring_in.at[s], ring_recv.at[s])
                ring_now[...] = ring_in[s]
                rings = [ring_terms(k) for k in range(K)]
                wait_all(edge_in.at[s, pl.ds(0, tiles - 1), pl.ds(0, 1)], edge_recv.at[s])
                edge_now[:, 0:1] = edge_in[s, :, 0:1]
                edge_now[tile, 0:1] = edge_out[s, 0:1]
                sides = [next_sides(k, owns[k], rings[k]) for k in range(K)]
                for k in range(K):
                    keep(ghosts.at[1], k, sides[k])

        for k in range(K):
            slot = pl.ds(k * FINE_ROWS, FINE_ROWS)
            live = jnp.full((FINE_ROWS, width), lives[k], jnp.int32) > 0
            for f in range(3):
                out_ref[0, f, slot] = jnp.where(live, st[f, slot], state_ref[0, f, slot])

        for s in range(STEPS):
            wait_all(ret_in.at[s], ret_send.at[s])
        for s in range(STEPS - 1):
            wait_all(edge_in.at[s, pl.ds(0, tiles - 1), pl.ds(0, 1)], edge_send.at[s])


def on_device(n_row, n_nest, ocean_state, face_depth, face_open, nest_place, nest_host):
    tiles = n_row * n_nest
    height, width = ocean_state.shape[2:]
    f32 = jnp.float32
    vmem = pl.BlockSpec(memory_space=pltpu.VMEM)
    hbm = pl.BlockSpec(memory_space=pl.ANY)
    smem = pl.BlockSpec(memory_space=pltpu.SMEM)
    dma = pltpu.SemaphoreType.DMA
    return pl.pallas_call(
        functools.partial(kernel, n_row, n_nest),
        out_shape=jax.ShapeDtypeStruct(ocean_state.shape, f32),
        in_specs=[smem, smem, hbm, hbm, hbm],
        out_specs=vmem,
        scratch_shapes=[
            pltpu.VMEM(ocean_state.shape, f32),
            pltpu.VMEM(face_depth.shape, f32),
            pltpu.VMEM(face_open.shape, jnp.int32),
            dma((3,)),
            pltpu.VMEM((3, height, width), f32),
            pltpu.VMEM((6, height, width), f32),
            pltpu.VMEM((2, PH, width), f32),
            pltpu.VMEM((tiles, 2, PH, width), f32),
            pltpu.VMEM((PH, width), f32),
            pltpu.VMEM((tiles, PH, width), f32),
            pltpu.VMEM((STEPS - 1, PH, width), f32),
            pltpu.VMEM((STEPS - 1, tiles, PH, width), f32),
            pltpu.VMEM((STEPS - 1, PH, width), f32),
            pltpu.VMEM((STEPS - 1, tiles, PH, width), f32),
            pltpu.VMEM((STEPS, K, PH, width), f32),
            pltpu.VMEM((STEPS, tiles * K, PH, width), f32),
            pltpu.VMEM((STEPS, 8, width), f32),
            pltpu.VMEM((STEPS, 8, width), f32),
            pltpu.VMEM((STEPS, 8, width), f32),
            pltpu.VMEM((STEPS, 8, width), f32),
            pltpu.VMEM((STEPS, 8, width), f32),
            pltpu.VMEM((STEPS, 8, width), f32),
            pltpu.VMEM((STEPS, 8, width), f32),
            pltpu.VMEM((STEPS, 8, width), f32),
            pltpu.VMEM((K, width, width), jnp.bfloat16),
            pltpu.VMEM((2, K, FINE_ROWS + 8, width), f32),
            pltpu.VMEM((tiles, PH, width), f32),
            pltpu.VMEM((tiles, PH, width), f32),
            pltpu.VMEM((tiles * K, PH, width), f32),
            pltpu.VMEM((K, FINE_ROWS + 8, width), f32),
            dma((2,)),
            dma((2,)),
            dma((STEPS - 1,)),
            dma((STEPS - 1,)),
            dma((STEPS - 1,)),
            dma((STEPS - 1,)),
            dma((STEPS,)),
            dma((STEPS,)),
            dma((STEPS, 4)),
            dma((STEPS, 4)),
        ],
        compiler_params=pltpu.CompilerParams(collective_id=0, has_side_effects=True),
    )(nest_place, nest_host, ocean_state, face_depth, face_open)


def solution(mesh):
    field = P("sec", None, "row", "nest")
    return jax.shard_map(
        functools.partial(on_device, mesh.shape["row"], mesh.shape["nest"]),
        mesh=mesh,
        in_specs=(field, field, field, P(), P()),
        out_specs=field,
        check_vma=False,
    )
```
